256 devices in a mesh: seq: 32 (over z, x), head: 8 (over y, core).
Axes of the slice: x: 4, y: 4, z: 8, core: 2. Of those that a mesh axis runs over, the one named last changes fastest.
Arguments:
- queries: bfloat16 [16384, 4096], P('seq', 'head'), may hold values from -0.3984375 to 0.3984375
- keys: bfloat16 [16384, 4096], P('seq', 'head'), may hold values from -0.3984375 to 0.3984375
- values: bfloat16 [16384, 1024], P('seq', 'head'), may hold values from -3 to 3
- out_grad: bfloat16 [16384, 1024], P('seq', 'head'), may hold values from -0.29882812 to 0.29882812
- transitions: bfloat16 [32, 256, 256], replicated, may hold values from -1 to 1, as said below
- gammas: float32 [16], P('head'), may hold values from 0.6 to 1
- regimes: int32 [64], replicated, may hold values from 0 to 31
- documents: int32 [64], replicated, may hold values from 0 to 7, never falling along the last dimension, each value on 1 to 32 neighbouring positions
Outputs:
- query_grad: bfloat16 [16384, 4096], P('seq', 'head')
- key_grad: bfloat16 [16384, 4096], P('seq', 'head')
- value_grad: bfloat16 [16384, 1024], P('seq', 'head')
- regime_grad: float32 [32, 256, 256], P('seq', 'head')
The draws below stay inside these ranges and needn't reach their ends.
Inputs may be any that keep to these rules, and one draw needn't show every extreme that they name: `transitions`: diagonal entries lie in 0.9 to 1.0, the others are small. `documents`: document numbers never fall; each document spans at most 32 blocks and one spans exactly that many.
All inputs are finite; a program needn't handle non-finite values.
Results may differ from the reference program's by a relative error of at most 0.005.
Values sent between devices are 32-bit elements; how exact they have to be, the bound alone decides.
A program may use at most 64 MiB of HBM per device.

```python
import math
import jax
import jax.numpy as jnp
import numpy as np
from jax import lax

STATE = 256
HEADS = 16
HEAD_DIM = 64
REGIMES = 32
BLOCK = 256
TOKENS = 16384
BLOCKS = 64
DOCS = 8


def draw_transitions(key, part):
    diagonal_key, remainder_key = jax.random.split(key)
    diagonal = jax.random.uniform(diagonal_key, (REGIMES, STATE, 1), jnp.float32, 0.9, 1.0)
    spread = 0.2 / math.sqrt(STATE)
    remainder = jnp.clip(jax.random.normal(remainder_key, (REGIMES, STATE, STATE), jnp.float32) * spread, -4.0 * spread, 4.0 * spread)
    on_diagonal = lax.broadcasted_iota(jnp.int32, (STATE, STATE), 0) == lax.broadcasted_iota(jnp.int32, (STATE, STATE), 1)
    return jnp.where(on_diagonal[None], diagonal, remainder).astype(jnp.bfloat16)


def touch_ends(result, stream_key, low, largest):
    longest = result.shape.index(max(result.shape))
    spots = []
    for shift in (0, 1):
        where = [jax.random.randint(jax.random.fold_in(stream_key, axis), (), 0, length) for axis, length in enumerate(result.shape)]
        where[longest] = (where[longest] + shift) % result.shape[longest]
        spots.append(tuple(where))
    return result.at[spots[0]].set(low).at[spots[1]].set(largest)


def levels(key, extent, pieces, least, top_value):
    level = 1.0
    for axis_at, parts in pieces:
        heights = jax.random.uniform(jax.random.fold_in(jax.random.fold_in(key, 6), axis_at), (parts,), jnp.float32, least / len(pieces), top_value / len(pieces))
        level = level * jnp.repeat(jnp.exp(heights), extent[axis_at] // parts).reshape((-1,) + (1,) * (len(extent) - 1 - axis_at))
    return level


def split_up(number_of, total, most, lean):
    weights = [(1 << 20) // math.isqrt(grade ** lean) + 1 for grade in range(2, number_of + 1)]
    rest, counts = total - most - (number_of - 1), [1] * (number_of - 1)
    while rest > 0:
        movable = [i for i in range(number_of - 1) if counts[i] < most]
        whole, remaining = sum([weights[i] for i in movable]), rest
        for i in movable:
            addition = min(most - counts[i], max(1, remaining * weights[i] // whole), rest)
            counts[i] = counts[i] + addition
            rest = rest - addition
    return np.array([most] + counts)


def ragged(rng, count, total, limit, lean):
    if count == 2:
        one = jax.random.randint(rng, (), max(1, total - limit), min(limit, total - 1) + 1)
        return jnp.stack([one, total - one])
    tallies = jnp.asarray(split_up(count, total, limit, lean), jnp.int32)
    pairs = (count - 1) // 2
    donor, receiver = tallies[1:1 + 2 * pairs:2], tallies[2:2 + 2 * pairs:2]
    margin = jnp.minimum(donor - 1, limit - receiver)
    moved = jax.random.randint(jax.random.fold_in(rng, 1), (pairs,), 0, 1 << 20) % (margin + 1)
    tallies = tallies.at[1:1 + 2 * pairs:2].set(donor - moved).at[2:2 + 2 * pairs:2].set(receiver + moved)
    return tallies[jax.random.permutation(jax.random.fold_in(rng, 2), count)]


def bell_draw(own_key, extent, deviation, reach, pieces=(), kind=jnp.bfloat16):
    values = jax.random.normal(own_key, extent, jnp.float32) * deviation
    if len(pieces) > 0:
        values = levels(own_key, extent, pieces, -0.22, 0.18) * values
    return jnp.clip(values, min=-reach, max=reach).astype(kind)


def setup_inputs(seed: int = 0) -> dict:
    splits = jax.random.split(jax.random.key(seed), 9)
    queries = bell_draw(splits[0], (TOKENS, HEADS * STATE), 0.0625, 0.3984375, ((0, 32), (1, 8)))
    keys = bell_draw(splits[1], (TOKENS, HEADS * STATE), 0.0625, 0.3984375, ((0, 32), (1, 8)))
    values = bell_draw(splits[2], (TOKENS, HEADS * HEAD_DIM), 0.5, 3.0, ((0, 32), (1, 8)))
    out_grad = bell_draw(splits[3], (TOKENS, HEADS * HEAD_DIM), 0.05, 0.29882812, ((0, 32), (1, 8)))
    transitions = draw_transitions(jax.random.fold_in(splits[8], 71), 0)
    gammas = jnp.clip(jnp.exp(math.log(1.0) - 0.5108256 * jax.random.uniform(splits[5], (HEADS,), jnp.float32) ** levels(splits[5], (HEADS,), ((0, 8),), -0.2, 0.2)), 0.6, 1.0)
    regimes = touch_ends(jax.random.randint(splits[6], (BLOCKS,), 0, REGIMES), jax.random.fold_in(splits[6], 1), 0, REGIMES - 1).astype(jnp.int32)
    documents = jnp.searchsorted(jnp.cumsum(ragged(splits[7], DOCS, BLOCKS, BLOCKS // 2, 1)), jnp.arange(BLOCKS), side="right").astype(jnp.int32)
    return dict(queries=queries, keys=keys, values=values, out_grad=out_grad, transitions=transitions, gammas=gammas, regimes=regimes, documents=documents)


PRECISE = lax.Precision.HIGHEST


def rounded(array):
    return lax.optimization_barrier(array.astype(jnp.bfloat16)).astype(jnp.float32)


def reference(queries, keys, values, out_grad, transitions, gammas, regimes, documents):
    query_rows = queries.reshape(BLOCKS, BLOCK, HEADS, STATE).astype(jnp.float32)
    key_rows = keys.reshape(BLOCKS, BLOCK, HEADS, STATE).astype(jnp.float32)
    value_rows = values.reshape(BLOCKS, BLOCK, HEADS, HEAD_DIM).astype(jnp.float32)
    grad_rows = out_grad.reshape(BLOCKS, BLOCK, HEADS, HEAD_DIM).astype(jnp.float32)
    same_doc = (documents[1:] == documents[:-1]).astype(jnp.float32)
    kept = jnp.concatenate([jnp.zeros((1,), jnp.float32), same_doc])
    matrices = jnp.take(transitions, regimes, axis=0).astype(jnp.float32)
    decays = gammas.astype(jnp.float32)
    zero_state = jnp.zeros((HEADS, STATE, HEAD_DIM), jnp.float32)

    def forward(previous, inputs):
        matrix, keep_one, key_block, value_block = inputs
        factor = keep_one * decays
        entry = factor[:, None, None] * jnp.einsum("nm,hmp->hnp", matrix, previous, precision=PRECISE)
        update = jnp.einsum("lhn,lhp->hnp", key_block, value_block, precision=PRECISE)
        return entry + update, (entry, previous)

    _, (entries, befores) = lax.scan(forward, zero_state, (matrices, kept, key_rows, value_rows))

    def backward(carried, inputs):
        matrix, keep_one, query_block, grad_block = inputs
        total = jnp.einsum("lhn,lhp->hnp", query_block, grad_block, precision=PRECISE) + carried
        factor = keep_one * decays
        passed = factor[:, None, None] * jnp.einsum("nm,hnp->hmp", matrix, total, precision=PRECISE)
        return passed, (total, carried)

    _, (totals, leaving) = lax.scan(backward, zero_state, (matrices, kept, query_rows, grad_rows), reverse=True)

    terms = kept[:, None, None] * jnp.einsum("h,chnp,chmp->cnm", decays, totals, befores, precision=PRECISE)
    regime_grad = jax.ops.segment_sum(terms, regimes, num_segments=REGIMES)

    causal = jnp.arange(BLOCK)[:, None] >= jnp.arange(BLOCK)[None, :]

    def within(inputs):
        query_block, key_block, value_block, grad_block, entry, leave = inputs
        scores = jnp.einsum("lhn,shn->hls", query_block, key_block, precision=PRECISE)
        probs = rounded(jnp.where(causal[None], scores, 0.0))
        dots = jnp.einsum("lhp,shp->hls", grad_block, value_block, precision=PRECISE)
        dscore = rounded(jnp.where(causal[None], dots, 0.0))
        entry_b = rounded(entry)
        leave_b = rounded(leave)
        query_grad = jnp.einsum("lhp,hnp->lhn", grad_block, entry_b, precision=PRECISE) + jnp.einsum("hls,shn->lhn", dscore, key_block, precision=PRECISE)
        key_grad = jnp.einsum("shp,hnp->shn", value_block, leave_b, precision=PRECISE) + jnp.einsum("hls,lhn->shn", dscore, query_block, precision=PRECISE)
        value_grad = jnp.einsum("shn,hnp->shp", key_block, leave_b, precision=PRECISE) + jnp.einsum("hls,lhp->shp", probs, grad_block, precision=PRECISE)
        return (query_grad.astype(jnp.bfloat16), key_grad.astype(jnp.bfloat16), value_grad.astype(jnp.bfloat16))

    query_grad, key_grad, value_grad = lax.map(within, (query_rows, key_rows, value_rows, grad_rows, entries, leaving))
    return (query_grad.reshape(TOKENS, HEADS * STATE), key_grad.reshape(TOKENS, HEADS * STATE), value_grad.reshape(TOKENS, HEADS * HEAD_DIM), regime_grad)
```

```python
import functools

import jax
import jax.numpy as jnp
from jax import lax
from jax.experimental import pallas as pl
from jax.experimental.pallas import tpu as pltpu
from jax.sharding import PartitionSpec as P

BLOCK = 256
STATE = 256
HEAD_DIM = 64
HEADS_DEV = 2
X = 4
CORES = 2
BACK = 4
MESH = pl.DeviceIdType.MESH
F32 = jnp.float32
BF16 = jnp.bfloat16
NN = (((1,), (0,)), ((), ()))
NT = (((1,), (1,)), ((), ()))
TN = (((0,), (0,)), ((), ()))


def dot(a, b, dims):
    return lax.dot_general(a, b, dims, preferred_element_type=F32)


def split(a):
    high = a.astype(BF16)
    return high, (a - high.astype(F32)).astype(BF16)


def turn(state, matrix, dims):
    rows = state.shape[0]
    both = dot(jnp.concatenate(split(state), axis=0), matrix, dims)
    return both[:rows] + both[rows:]


def turn_split(state, high, low, dims):
    rows = state.shape[0]
    state_high, state_low = split(state)
    both = dot(jnp.concatenate([state_high, state_low], axis=0), high, dims)
    return both[:rows] + both[rows:] + dot(state_high, low, dims)


def product(a, b):
    a_high, a_low = a
    b_high, b_low = b
    return dot(a_high, b_high, NN) + (dot(a_high, b_low, NN) + dot(a_low, b_high, NN))


def kernel(
    sizes,
    regimes,
    documents,
    gammas,
    q_hbm,
    k_hbm,
    v_hbm,
    g_hbm,
    t_hbm,
    qo_hbm,
    ko_hbm,
    vo_hbm,
    ro_hbm,
    q,
    k,
    v,
    g,
    mats,
    qo,
    ko,
    vo,
    ro,
    q_part,
    k_part,
    v_part,
    update,
    source,
    pairs,
    groups,
    inner,
    t_send,
    t_recv,
    z_send,
    z_fwd,
    z_bwd,
    s_send,
    s_recv,
    terms,
    h_core,
    h_sum,
    h_y,
    h_block,
    h_x,
    h_reg,
    h_z,
    in_sem,
    out_sem,
    send_sem,
    recv_sem,
):
    Z, Y, N, HD, B = sizes
    rows = HEADS_DEV * HD
    piece = rows // X
    seq = lax.axis_index("seq")
    head = lax.axis_index("head")
    z, x = seq // X, seq % X
    y, core = head // CORES, head % CORES

    def at(dz, dx, dy, dc):
        where = ((z + dz) % Z * X + (x + dx) % X, (y + dy) % Y * CORES + (core + dc) % CORES)
        return where

    loads = [
        pltpu.make_async_copy(src, dst, in_sem.at[i])
        for i, (src, dst) in enumerate(
            [(k_hbm, k), (v_hbm, v), (g_hbm, g), (q_hbm, q), (t_hbm, mats)]
        )
    ]
    for load in loads:
        load.start()

    peers = (
        [at(0, j, 0, 0) for j in range(1, X)]
        + [at(j, 0, 0, 0) for j in range(1, Z)]
        + [at(0, 0, j, 0) for j in range(1, Y)]
        + [at(0, 0, 0, 1)]
    )
    barrier = pltpu.get_barrier_semaphore()
    for peer in peers:
        pl.semaphore_signal(barrier, inc=1, device_id=peer, device_id_type=MESH)

    used = [0]

    def send(src, dst, peer):
        number = used[0]
        used[0] += 1
        return pltpu.make_async_remote_copy(
            src_ref=src,
            dst_ref=dst,
            send_sem=send_sem.at[number],
            recv_sem=recv_sem.at[number],
            device_id=peer,
            device_id_type=MESH,
        )

    def kept(c):
        same = documents[c] == documents[jnp.maximum(c - 1, 0)]
        return jnp.where(same, 1.0, 0.0).astype(F32) * jnp.where(c > 0, 1.0, 0.0).astype(F32)

    def matrix(c):
        return mats[regimes[c]]

    row_id = lax.broadcasted_iota(jnp.int32, (rows, 1), 0)
    gamma_rows = jnp.where(row_id < HD, gammas[0], gammas[1])
    lane_id = lax.broadcasted_iota(jnp.int32, (1, rows), 1)
    lane_mask = [lane_id < HD, lane_id >= HD]
    first = seq * 2
    keep = [kept(first), kept(first + 1)]

    def tokens(b):
        return slice(b * B, (b + 1) * B)

    def lanes(h):
        return slice(h * N, (h + 1) * N)

    loads[0].wait()
    loads[1].wait()
    for b in range(2):
        flipped = v[tokens(b), :].T
        for h in range(HEADS_DEV):
            part = slice(h * HD, (h + 1) * HD)
            update[b, part, :] = dot(flipped[part], k[tokens(b), lanes(h)], NN)
    loads[2].wait()
    loads[3].wait()
    for b in range(2):
        flipped = g[tokens(b), :].T
        for h in range(HEADS_DEV):
            part = slice(h * HD, (h + 1) * HD)
            source[b, part, :] = dot(flipped[part], q[tokens(b), lanes(h)], NN)
    loads[4].wait()
    m0 = matrix(first)
    m1 = matrix(first + 1)
    ahead = update[1] + keep[1] * gamma_rows * turn(update[0], m1, NT)
    behind = source[0] + keep[1] * gamma_rows * turn(source[1], m1, NN)
    behind = keep[0] * gamma_rows * turn(behind, m0, NN)
    for j in range(X):
        part = slice(j * piece, (j + 1) * piece)
        t_send[j, 0] = ahead[part]
        t_send[j, 1] = behind[part]

    pl.semaphore_wait(barrier, len(peers))
    first_round = [
        send(t_send.at[(x + j) % X], t_recv.at[x], at(0, j, 0, 0)) for j in range(1, X)
    ]
    for copy in first_round:
        copy.start()
    t_recv[x] = t_send[x]

    def pair_product(c):
        return dot(matrix(c + 1), matrix(c), NN)

    base = z * 2 * X
    for j in range(X):
        high, low = split(pair_product(base + 2 * j))
        pairs[j, 0] = high
        pairs[j, 1] = low

    def pair(j):
        return pairs[j, 0], pairs[j, 1]

    def group_product(number, offset):
        group = (z + offset + Z) % Z
        made = [split(pair_product(group * 2 * X + 2 * j)) for j in range(X)]
        while len(made) > 1:
            made = [split(product(made[i + 1], made[i])) for i in range(0, len(made), 2)]
        groups[number, 0] = made[0][0]
        groups[number, 1] = made[0][1]

    @pl.loop(0, BACK - 1)
    def _(i):
        group_product(i, -1 - i)

    gamma = gammas[(x * piece) // HD]
    gamma2 = gamma * gamma
    scale = [gamma2 * kept(base + 2 * j) * kept(base + 2 * j + 1) for j in range(X)]

    for copy in first_round:
        copy.wait()
    run = t_recv[0, 0]
    before = [None, run]
    for j in range(1, X):
        run = t_recv[j, 0] + scale[j] * turn_split(run, *pair(j), NT)
        before.append(run)
    run = t_recv[X - 1, 1]
    after = [None] * X
    for j in reversed(range(X - 1)):
        after[j] = run
        run = t_recv[j, 1] + scale[j] * turn_split(run, *pair(j), NN)
    z_send[0] = before[X]
    z_send[1] = run
    second_round = []
    for j in range(1, BACK + 1):
        second_round.append(send(z_send.at[0], z_fwd.at[j - 1], at(j, 0, 0, 0)))
        second_round.append(send(z_send.at[1], z_bwd.at[j - 1], at(-j + Z, 0, 0, 0)))
    for copy in second_round:
        copy.start()

    @pl.loop(0, BACK - 1)
    def _(i):
        group_product(BACK - 1 + i, 1 + i)

    made = pair(0)
    for j in range(1, X - 1):
        made = split(product(pair(j), made))
        inner[0, j - 1, 0] = made[0]
        inner[0, j - 1, 1] = made[1]
    made = pair(X - 1)
    for j in reversed(range(1, X - 1)):
        made = split(product(made, pair(j)))
        inner[1, j - 1, 0] = made[0]
        inner[1, j - 1, 1] = made[1]

    row = lax.broadcasted_iota(jnp.int32, (B, B), 0)
    column = lax.broadcasted_iota(jnp.int32, (B, B), 1)
    for b in range(2):
        for h in range(HEADS_DEV):
            q_block = q[tokens(b), lanes(h)]
            k_block = k[tokens(b), lanes(h)]
            v_block = v[tokens(b), :]
            g_block = g[tokens(b), :]
            zero = jnp.zeros_like(g_block)
            g_head = jnp.where(lane_mask[h], g_block, zero)
            probs = jnp.where(row <= column, dot(k_block, q_block, NT), 0.0).astype(BF16)
            scored = jnp.where(row >= column, dot(g_head, v_block, NT), 0.0).astype(BF16)
            turned = jnp.where(row <= column, dot(v_block, g_head, NT), 0.0).astype(BF16)
            q_part[tokens(b), lanes(h)] = dot(scored, k_block, NN)
            k_part[tokens(b), lanes(h)] = dot(turned, q_block, NN)
            if h == 0:
                v_part[tokens(b), :] = dot(probs, g_head, NN)
            else:
                v_part[tokens(b), :] += dot(probs, g_head, NN)

    gamma_group = jnp.float32(1.0)
    for j in range(X):
        gamma_group = gamma_group * gamma2

    def group_scale(offset):
        group = (z + offset + Z) % Z
        total = gamma_group
        for j in range(2 * X):
            total = total * kept(group * 2 * X + j)
        return total

    for copy in second_round:
        copy.wait()
    inbound = z_fwd[BACK - 1]
    outbound = z_bwd[BACK - 1]
    for j in reversed(range(BACK - 1)):
        inbound = z_fwd[j] + group_scale(-1 - j) * turn_split(
            inbound, groups[j, 0], groups[j, 1], NT
        )
        outbound = z_bwd[j] + group_scale(1 + j) * turn_split(
            outbound, groups[BACK - 1 + j, 0], groups[BACK - 1 + j, 1], NN
        )
    s_send[0, 0] = inbound
    total_scale = scale[0]
    for j in range(1, X):
        made = pair(0) if j == 1 else (inner[0, j - 2, 0], inner[0, j - 2, 1])
        s_send[j, 0] = before[j] + total_scale * turn_split(inbound, *made, NT)
        total_scale = total_scale * scale[j]
    s_send[X - 1, 1] = outbound
    total_scale = scale[X - 1]
    for j in reversed(range(X - 1)):
        made = pair(X - 1) if j == X - 2 else (inner[1, j, 0], inner[1, j, 1])
        s_send[j, 1] = after[j] + total_scale * turn_split(outbound, *made, NN)
        total_scale = total_scale * scale[j]
    third_round = [
        send(s_send.at[(x + j) % X], s_recv.at[x], at(0, j, 0, 0)) for j in range(1, X)
    ]
    for copy in third_round:
        copy.start()
    s_recv[x] = s_send[x]
    for copy in third_round:
        copy.wait()

    previous = jnp.concatenate([s_recv[j, 0] for j in range(X)], axis=0)
    leaving = jnp.concatenate([s_recv[j, 1] for j in range(X)], axis=0)
    total1 = source[1] + leaving
    entry0 = keep[0] * gamma_rows * turn(previous, m0, NT)
    leave0 = keep[1] * gamma_rows * turn(total1, m1, NN)
    end0 = entry0 + update[0]
    total0 = source[0] + leave0
    for b, (left, right) in enumerate([(total0, previous), (total1, end0)]):
        left_high, left_low = split(left * (keep[b] * gamma_rows))
        right_high, right_low = split(right)
        term = dot(
            jnp.concatenate([left_high, left_low, left_high], axis=0),
            jnp.concatenate([right_high, right_high, right_low], axis=0),
            TN,
        )
        height = N // (Y * CORES)
        for j in range(Y * CORES):
            terms[j % CORES, j // CORES, b] = term[j * height : (j + 1) * height]
    core_copy = send(terms.at[1 - core], h_core, at(0, 0, 0, 1))
    core_copy.start()

    entry1 = keep[1] * gamma_rows * turn(end0, m1, NT)
    entries = [entry0.astype(BF16), entry1.astype(BF16)]
    leaves = [leave0.astype(BF16), leaving.astype(BF16)]

    core_copy.wait()
    for j in range(Y):
        h_sum[j] = terms[core, j] + h_core[j]
    y_round = [send(h_sum.at[(y + j) % Y], h_y.at[j - 1], at(0, 0, j, 0)) for j in range(1, Y)]
    for copy in y_round:
        copy.start()

    stores = []
    for b in range(2):
        v_block = v[tokens(b), :]
        g_block = g[tokens(b), :]
        zero = jnp.zeros_like(g_block)
        v_new = v_part[tokens(b), :]
        for h in range(HEADS_DEV):
            g_head = jnp.where(lane_mask[h], g_block, zero)
            v_head = jnp.where(lane_mask[h], v_block, zero)
            qo[tokens(b), lanes(h)] = (
                q_part[tokens(b), lanes(h)] + dot(g_head, entries[b], NN)
            ).astype(BF16)
            ko[tokens(b), lanes(h)] = (
                k_part[tokens(b), lanes(h)] + dot(v_head, leaves[b], NN)
            ).astype(BF16)
            v_new = v_new + jnp.where(
                lane_mask[h], dot(k[tokens(b), lanes(h)], leaves[b], NT), 0.0
            )
        vo[tokens(b), :] = v_new.astype(BF16)
    for i, (src, dst) in enumerate([(qo, qo_hbm), (ko, ko_hbm), (vo, vo_hbm)]):
        stores.append(pltpu.make_async_copy(src, dst, out_sem.at[i]))
        stores[-1].start()

    for copy in y_round:
        copy.wait()
    mine = h_sum[y]
    for j in range(Y - 1):
        mine = mine + h_y[j]
    h_block[...] = mine
    x_round = [send(h_block, h_x.at[x], at(0, j, 0, 0)) for j in range(1, X)]
    for copy in x_round:
        copy.start()
    h_x[x] = mine
    for copy in x_round:
        copy.wait()
    for j in range(Z):
        owner = (z + j) % Z * X + x
        total = jnp.zeros_like(ro[...])
        for i in range(2 * X):
            chosen = jnp.where(regimes[base + i] == owner, 1.0, 0.0).astype(F32)
            total = total + chosen * h_x[i // 2, i % 2]
        h_reg[j] = total
    z_round = [send(h_reg.at[j], h_z.at[j - 1], at(j, 0, 0, 0)) for j in range(1, Z)]
    for copy in z_round:
        copy.start()
    for copy in z_round:
        copy.wait()
    final = h_reg[0]
    for j in range(Z - 1):
        final = final + h_z[j]
    ro[...] = final
    last = pltpu.make_async_copy(ro, ro_hbm.at[0], out_sem.at[3])
    last.start()
    for store in stores:
        store.wait()
    last.wait()


def local(Z, Y, queries, keys, values, out_grad, transitions, gammas, regimes, documents):
    tokens_dev = queries.shape[0]
    N = transitions.shape[1]
    rows = values.shape[1]
    HD = rows // HEADS_DEV
    B = tokens_dev // 2
    piece = rows // X
    height = N // (Y * CORES)
    anywhere = pl.BlockSpec(memory_space=pl.ANY)
    scalar = pl.BlockSpec(memory_space=pltpu.SMEM)
    vmem = pltpu.VMEM
    copies = 3 * (X - 1) + 2 * BACK + 1 + (Y - 1) + (Z - 1)
    return pl.pallas_call(
        functools.partial(kernel, (Z, Y, N, HD, B)),
        out_shape=(
            jax.ShapeDtypeStruct(queries.shape, BF16),
            jax.ShapeDtypeStruct(keys.shape, BF16),
            jax.ShapeDtypeStruct(values.shape, BF16),
            jax.ShapeDtypeStruct((1, height, N), F32),
        ),
        in_specs=[scalar] * 3 + [anywhere] * 5,
        out_specs=[anywhere] * 4,
        scratch_shapes=[
            vmem(queries.shape, BF16),
            vmem(keys.shape, BF16),
            vmem(values.shape, BF16),
            vmem(values.shape, BF16),
            vmem(transitions.shape, BF16),
            vmem(queries.shape, BF16),
            vmem(keys.shape, BF16),
            vmem(values.shape, BF16),
            vmem((height, N), F32),
            vmem(queries.shape, F32),
            vmem(keys.shape, F32),
            vmem(values.shape, F32),
            vmem((2, rows, N), F32),
            vmem((2, rows, N), F32),
            vmem((X, 2, N, N), BF16),
            vmem((2 * (BACK - 1), 2, N, N), BF16),
            vmem((2, X - 2, 2, N, N), BF16),
            vmem((X, 2, piece, N), F32),
            vmem((X, 2, piece, N), F32),
            vmem((2, piece, N), F32),
            vmem((BACK, piece, N), F32),
            vmem((BACK, piece, N), F32),
            vmem((X, 2, piece, N), F32),
            vmem((X, 2, piece, N), F32),
            vmem((CORES, Y, 2, height, N), F32),
            vmem((Y, 2, height, N), F32),
            vmem((Y, 2, height, N), F32),
            vmem((Y - 1, 2, height, N), F32),
            vmem((2, height, N), F32),
            vmem((X, 2, height, N), F32),
            vmem((Z, height, N), F32),
            vmem((Z - 1, height, N), F32),
            pltpu.SemaphoreType.DMA((5,)),
            pltpu.SemaphoreType.DMA((4,)),
            pltpu.SemaphoreType.DMA((copies,)),
            pltpu.SemaphoreType.DMA((copies,)),
        ],
        compiler_params=pltpu.CompilerParams(collective_id=0, has_side_effects=True),
        name="whole",
    )(regimes, documents, gammas, queries, keys, values, out_grad, transitions)


def solution(mesh):
    in_specs = (
        P("seq", "head"),
        P("seq", "head"),
        P("seq", "head"),
        P("seq", "head"),
        P(),
        P("head"),
        P(),
        P(),
    )
    out_specs = (P("seq", "head"), P("seq", "head"), P("seq", "head"), P("seq", "head", None))
    body = functools.partial(local, mesh.shape["seq"] // X, mesh.shape["head"] // CORES)
    return jax.shard_map(body, mesh=mesh, in_specs=in_specs, out_specs=out_specs, check_vma=False)
```

```python
import functools

import jax
import jax.numpy as jnp
from jax import lax
from jax.experimental import pallas as pl
from jax.experimental.pallas import tpu as pltpu
from jax.sharding import PartitionSpec as P

BLOCK = 256
STATE = 256
HEAD_DIM = 64
HEADS_DEV = 2
X = 4
CORES = 2
BACK = 4
PARTS = 2
MESH = pl.DeviceIdType.MESH
F32 = jnp.float32
BF16 = jnp.bfloat16
NN = (((1,), (0,)), ((), ()))
NT = (((1,), (1,)), ((), ()))
TN = (((0,), (0,)), ((), ()))


def dot(a, b, dims):
    return lax.dot_general(a, b, dims, preferred_element_type=F32)


def split(a):
    high = a.astype(BF16)
    return high, (a - high.astype(F32)).astype(BF16)


def turn(state, matrix, dims):
    rows = state.shape[0]
    both = dot(jnp.concatenate(split(state), axis=0), matrix, dims)
    return both[:rows] + both[rows:]


def turn_split(state, high, low, dims):
    rows = state.shape[0]
    state_high, state_low = split(state)
    both = dot(jnp.concatenate([state_high, state_low], axis=0), high, dims)
    return both[:rows] + both[rows:] + dot(state_high, low, dims)


def product(a, b):
    a_high, a_low = a
    b_high, b_low = b
    return dot(a_high, b_high, NN) + (dot(a_high, b_low, NN) + dot(a_low, b_high, NN))


def kernel(
    sizes,
    regimes,
    documents,
    gammas,
    q_hbm,
    k_hbm,
    v_hbm,
    g_hbm,
    t_hbm,
    qo,
    ko,
    vo,
    ro,
    q,
    k,
    v,
    g,
    mats,
    q_part,
    k_part,
    v_part,
    update,
    source,
    pairs,
    groups,
    inner,
    t_send,
    t_recv,
    z_send,
    z_fwd,
    z_bwd,
    s_send,
    s_recv,
    terms,
    h_core,
    h_sum,
    h_y,
    h_block,
    h_x,
    h_reg,
    h_z,
    in_sem,
    send_sem,
    recv_sem,
):
    Z, Y, N, HD, B = sizes
    rows = HEADS_DEV * HD
    piece = rows // X
    seq = lax.axis_index("seq")
    head = lax.axis_index("head")
    z, x = seq // X, seq % X
    y, core = head // CORES, head % CORES

    def at(dz, dx, dy, dc):
        where = ((z + dz) % Z * X + (x + dx) % X, (y + dy) % Y * CORES + (core + dc) % CORES)
        return where

    loads = [
        pltpu.make_async_copy(src, dst, in_sem.at[i])
        for i, (src, dst) in enumerate(
            [(k_hbm, k), (v_hbm, v), (g_hbm, g), (q_hbm, q), (t_hbm, mats)]
        )
    ]
    for load in loads:
        load.start()

    peers = (
        [at(0, j, 0, 0) for j in range(1, X)]
        + [at(j, 0, 0, 0) for j in range(1, Z)]
        + [at(0, 0, j, 0) for j in range(1, Y)]
        + [at(0, 0, 0, 1)]
    )
    barrier = pltpu.get_barrier_semaphore()
    for peer in peers:
        pl.semaphore_signal(barrier, inc=1, device_id=peer, device_id_type=MESH)

    used = [0]

    def send(src, dst, peer):
        number = used[0]
        used[0] += 1
        return pltpu.make_async_remote_copy(
            src_ref=src,
            dst_ref=dst,
            send_sem=send_sem.at[number],
            recv_sem=recv_sem.at[number],
            device_id=peer,
            device_id_type=MESH,
        )

    def kept(c):
        same = documents[c] == documents[jnp.maximum(c - 1, 0)]
        return jnp.where(same, 1.0, 0.0).astype(F32) * jnp.where(c > 0, 1.0, 0.0).astype(F32)

    def matrix(c):
        return mats[regimes[c]]

    row_id = lax.broadcasted_iota(jnp.int32, (rows, 1), 0)
    gamma_rows = jnp.where(row_id < HD, gammas[0], gammas[1])
    lane_id = lax.broadcasted_iota(jnp.int32, (1, rows), 1)
    lane_mask = [lane_id < HD, lane_id >= HD]
    first = seq * 2
    keep = [kept(first), kept(first + 1)]

    def tokens(b):
        return slice(b * B, (b + 1) * B)

    def lanes(h):
        return slice(h * N, (h + 1) * N)

    loads[0].wait()
    loads[1].wait()
    for b in range(2):
        flipped = v[tokens(b), :].T
        for h in range(HEADS_DEV):
            part = slice(h * HD, (h + 1) * HD)
            update[b, part, :] = dot(flipped[part], k[tokens(b), lanes(h)], NN)
    loads[2].wait()
    loads[3].wait()
    for b in range(2):
        flipped = g[tokens(b), :].T
        for h in range(HEADS_DEV):
            part = slice(h * HD, (h + 1) * HD)
            source[b, part, :] = dot(flipped[part], q[tokens(b), lanes(h)], NN)
    loads[4].wait()
    m0 = matrix(first)
    m1 = matrix(first + 1)
    ahead = update[1] + keep[1] * gamma_rows * turn(update[0], m1, NT)
    behind = source[0] + keep[1] * gamma_rows * turn(source[1], m1, NN)
    behind = keep[0] * gamma_rows * turn(behind, m0, NN)
    for j in range(X):
        part = slice(j * piece, (j + 1) * piece)
        t_send[j, 0] = ahead[part]
        t_send[j, 1] = behind[part]

    pl.semaphore_wait(barrier, len(peers))
    first_round = [
        send(t_send.at[(x + j) % X], t_recv.at[x], at(0, j, 0, 0)) for j in range(1, X)
    ]
    for copy in first_round:
        copy.start()
    t_recv[x] = t_send[x]

    def pair_product(c):
        return dot(matrix(c + 1), matrix(c), NN)

    base = z * 2 * X
    for j in range(X):
        high, low = split(pair_product(base + 2 * j))
        pairs[j, 0] = high
        pairs[j, 1] = low

    def pair(j):
        return pairs[j, 0], pairs[j, 1]

    def group_product(number, offset):
        group = (z + offset + Z) % Z
        made = [split(pair_product(group * 2 * X + 2 * j)) for j in range(X)]
        while len(made) > 1:
            made = [split(product(made[i + 1], made[i])) for i in range(0, len(made), 2)]
        groups[number, 0] = made[0][0]
        groups[number, 1] = made[0][1]

    @pl.loop(0, BACK - 1)
    def _(i):
        group_product(i, -1 - i)

    gamma = gammas[(x * piece) // HD]
    gamma2 = gamma * gamma
    scale = [gamma2 * kept(base + 2 * j) * kept(base + 2 * j + 1) for j in range(X)]

    for copy in first_round:
        copy.wait()
    run = t_recv[0, 0]
    before = [None, run]
    for j in range(1, X):
        run = t_recv[j, 0] + scale[j] * turn_split(run, *pair(j), NT)
        before.append(run)
    run = t_recv[X - 1, 1]
    after = [None] * X
    for j in reversed(range(X - 1)):
        after[j] = run
        run = t_recv[j, 1] + scale[j] * turn_split(run, *pair(j), NN)
    z_send[0] = before[X]
    z_send[1] = run
    second_round = []
    for j in range(1, BACK + 1):
        second_round.append(send(z_send.at[0], z_fwd.at[j - 1], at(j, 0, 0, 0)))
        second_round.append(send(z_send.at[1], z_bwd.at[j - 1], at(-j + Z, 0, 0, 0)))
    for copy in second_round:
        copy.start()

    @pl.loop(0, BACK - 1)
    def _(i):
        group_product(BACK - 1 + i, 1 + i)

    made = pair(0)
    for j in range(1, X - 1):
        made = split(product(pair(j), made))
        inner[0, j - 1, 0] = made[0]
        inner[0, j - 1, 1] = made[1]
    made = pair(X - 1)
    for j in reversed(range(1, X - 1)):
        made = split(product(made, pair(j)))
        inner[1, j - 1, 0] = made[0]
        inner[1, j - 1, 1] = made[1]

    row = lax.broadcasted_iota(jnp.int32, (B, B), 0)
    column = lax.broadcasted_iota(jnp.int32, (B, B), 1)
    for b in range(2):
        for h in range(HEADS_DEV):
            q_block = q[tokens(b), lanes(h)]
            k_block = k[tokens(b), lanes(h)]
            v_block = v[tokens(b), :]
            g_block = g[tokens(b), :]
            zero = jnp.zeros_like(g_block)
            g_head = jnp.where(lane_mask[h], g_block, zero)
            probs = jnp.where(row <= column, dot(k_block, q_block, NT), 0.0).astype(BF16)
            scored = jnp.where(row >= column, dot(g_head, v_block, NT), 0.0).astype(BF16)
            turned = jnp.where(row <= column, dot(v_block, g_head, NT), 0.0).astype(BF16)
            q_part[tokens(b), lanes(h)] = dot(scored, k_block, NN)
            k_part[tokens(b), lanes(h)] = dot(turned, q_block, NN)
            if h == 0:
                v_part[tokens(b), :] = dot(probs, g_head, NN)
            else:
                v_part[tokens(b), :] += dot(probs, g_head, NN)

    gamma_group = jnp.float32(1.0)
    for j in range(X):
        gamma_group = gamma_group * gamma2

    def group_scale(offset):
        group = (z + offset + Z) % Z
        total = gamma_group
        for j in range(2 * X):
            total = total * kept(group * 2 * X + j)
        return total

    for copy in second_round:
        copy.wait()
    inbound = z_fwd[BACK - 1]
    outbound = z_bwd[BACK - 1]
    for j in reversed(range(BACK - 1)):
        inbound = z_fwd[j] + group_scale(-1 - j) * turn_split(
            inbound, groups[j, 0], groups[j, 1], NT
        )
        outbound = z_bwd[j] + group_scale(1 + j) * turn_split(
            outbound, groups[BACK - 1 + j, 0], groups[BACK - 1 + j, 1], NN
        )
    s_send[0, 0] = inbound
    total_scale = scale[0]
    for j in range(1, X):
        made = pair(0) if j == 1 else (inner[0, j - 2, 0], inner[0, j - 2, 1])
        s_send[j, 0] = before[j] + total_scale * turn_split(inbound, *made, NT)
        total_scale = total_scale * scale[j]
    s_send[X - 1, 1] = outbound
    total_scale = scale[X - 1]
    for j in reversed(range(X - 1)):
        made = pair(X - 1) if j == X - 2 else (inner[1, j, 0], inner[1, j, 1])
        s_send[j, 1] = after[j] + total_scale * turn_split(outbound, *made, NN)
        total_scale = total_scale * scale[j]
    third_round = [
        send(s_send.at[(x + j) % X], s_recv.at[x], at(0, j, 0, 0)) for j in range(1, X)
    ]
    for copy in third_round:
        copy.start()
    s_recv[x] = s_send[x]
    for copy in third_round:
        copy.wait()

    previous = jnp.concatenate([s_recv[j, 0] for j in range(X)], axis=0)
    leaving = jnp.concatenate([s_recv[j, 1] for j in range(X)], axis=0)
    total1 = source[1] + leaving
    entry0 = keep[0] * gamma_rows * turn(previous, m0, NT)
    leave0 = keep[1] * gamma_rows * turn(total1, m1, NN)
    end0 = entry0 + update[0]
    total0 = source[0] + leave0
    for b, (left, right) in enumerate([(total0, previous), (total1, end0)]):
        left_high, left_low = split(left * (keep[b] * gamma_rows))
        right_high, right_low = split(right)
        term = dot(
            jnp.concatenate([left_high, left_low, left_high], axis=0),
            jnp.concatenate([right_high, right_high, right_low], axis=0),
            TN,
        )
        height = N // (Y * CORES)
        width = N // PARTS
        for j in range(Y * CORES):
            for t in range(PARTS):
                terms[t, j % CORES, j // CORES, b] = term[
                    j * height : (j + 1) * height, t * width : (t + 1) * width
                ]
    core_round = [send(terms.at[t, 1 - core], h_core.at[t], at(0, 0, 0, 1)) for t in range(PARTS)]
    for copy in core_round:
        copy.start()

    entry1 = keep[1] * gamma_rows * turn(end0, m1, NT)
    entries = [entry0.astype(BF16), entry1.astype(BF16)]
    leaves = [leave0.astype(BF16), leaving.astype(BF16)]

    y_round = []
    for t in range(PARTS):
        core_round[t].wait()
        for j in range(Y):
            h_sum[t, j] = terms[t, core, j] + h_core[t, j]
        copies = [
            send(h_sum.at[t, (y + j) % Y], h_y.at[t, j - 1], at(0, 0, j, 0)) for j in range(1, Y)
        ]
        for copy in copies:
            copy.start()
        y_round.append(copies)
    x_round = []
    for t in range(PARTS):
        for copy in y_round[t]:
            copy.wait()
        mine = h_sum[t, y]
        for j in range(Y - 1):
            mine = mine + h_y[t, j]
        h_block[t] = mine
        copies = [send(h_block.at[t], h_x.at[t, x], at(0, j, 0, 0)) for j in range(1, X)]
        for copy in copies:
            copy.start()
        x_round.append(copies)
        h_x[t, x] = mine
    chosen = [
        [
            jnp.where(regimes[base + i] == (z + j) % Z * X + x, 1.0, 0.0).astype(F32)
            for i in range(2 * X)
        ]
        for j in range(Z)
    ]
    z_round = []
    for t in range(PARTS):
        for copy in x_round[t]:
            copy.wait()
        for j in range(Z):
            total = chosen[j][0] * h_x[t, 0, 0]
            for i in range(1, 2 * X):
                total = total + chosen[j][i] * h_x[t, i // 2, i % 2]
            h_reg[t, j] = total
        copies = [send(h_reg.at[t, j], h_z.at[t, j - 1], at(j, 0, 0, 0)) for j in range(1, Z)]
        for copy in copies:
            copy.start()
        z_round.append(copies)

    for b in range(2):
        v_block = v[tokens(b), :]
        g_block = g[tokens(b), :]
        zero = jnp.zeros_like(g_block)
        v_new = v_part[tokens(b), :]
        for h in range(HEADS_DEV):
            g_head = jnp.where(lane_mask[h], g_block, zero)
            v_head = jnp.where(lane_mask[h], v_block, zero)
            qo[tokens(b), lanes(h)] = (
                q_part[tokens(b), lanes(h)] + dot(g_head, entries[b], NN)
            ).astype(BF16)
            ko[tokens(b), lanes(h)] = (
                k_part[tokens(b), lanes(h)] + dot(v_head, leaves[b], NN)
            ).astype(BF16)
            v_new = v_new + jnp.where(
                lane_mask[h], dot(k[tokens(b), lanes(h)], leaves[b], NT), 0.0
            )
        vo[tokens(b), :] = v_new.astype(BF16)

    for t in range(PARTS):
        for copy in z_round[t]:
            copy.wait()
        total = h_reg[t, 0]
        for j in range(Z - 1):
            total = total + h_z[t, j]
        ro[0, :, t * width : (t + 1) * width] = total


def write(*refs):
    count = (len(refs) - 1) // 2
    sem = refs[-1]
    copies = [pltpu.make_async_copy(refs[i], refs[count + i], sem.at[i]) for i in range(count)]
    for copy in copies:
        copy.start()
    for copy in copies:
        copy.wait()


def local(Z, Y, queries, keys, values, out_grad, transitions, gammas, regimes, documents):
    tokens_dev = queries.shape[0]
    N = transitions.shape[1]
    rows = values.shape[1]
    HD = rows // HEADS_DEV
    B = tokens_dev // 2
    piece = rows // X
    height = N // (Y * CORES)
    anywhere = pl.BlockSpec(memory_space=pl.ANY)
    scalar = pl.BlockSpec(memory_space=pltpu.SMEM)
    vmem = pltpu.VMEM
    width = N // PARTS
    copies = 2 * (X - 1) + 2 * BACK + PARTS * (1 + (Y - 1) + (X - 1) + (Z - 1))
    results = pl.pallas_call(
        functools.partial(kernel, (Z, Y, N, HD, B)),
        out_shape=(
            vmem(queries.shape, BF16),
            vmem(keys.shape, BF16),
            vmem(values.shape, BF16),
            vmem((1, height, N), F32),
        ),
        in_specs=[scalar] * 3 + [anywhere] * 5,
        out_specs=[pl.BlockSpec(memory_space=vmem)] * 4,
        scratch_shapes=[
            vmem(queries.shape, BF16),
            vmem(keys.shape, BF16),
            vmem(values.shape, BF16),
            vmem(values.shape, BF16),
            vmem(transitions.shape, BF16),
            vmem(queries.shape, F32),
            vmem(keys.shape, F32),
            vmem(values.shape, F32),
            vmem((2, rows, N), F32),
            vmem((2, rows, N), F32),
            vmem((X, 2, N, N), BF16),
            vmem((2 * (BACK - 1), 2, N, N), BF16),
            vmem((2, X - 2, 2, N, N), BF16),
            vmem((X, 2, piece, N), F32),
            vmem((X, 2, piece, N), F32),
            vmem((2, piece, N), F32),
            vmem((BACK, piece, N), F32),
            vmem((BACK, piece, N), F32),
            vmem((X, 2, piece, N), F32),
            vmem((X, 2, piece, N), F32),
            vmem((PARTS, CORES, Y, 2, height, width), F32),
            vmem((PARTS, Y, 2, height, width), F32),
            vmem((PARTS, Y, 2, height, width), F32),
            vmem((PARTS, Y - 1, 2, height, width), F32),
            vmem((PARTS, 2, height, width), F32),
            vmem((PARTS, X, 2, height, width), F32),
            vmem((PARTS, Z, height, width), F32),
            vmem((PARTS, Z - 1, height, width), F32),
            pltpu.SemaphoreType.DMA((5,)),
            pltpu.SemaphoreType.DMA((copies,)),
            pltpu.SemaphoreType.DMA((copies,)),
        ],
        compiler_params=pltpu.CompilerParams(collective_id=0, has_side_effects=True),
        name="whole",
    )(regimes, documents, gammas, queries, keys, values, out_grad, transitions)
    return pl.pallas_call(
        write,
        out_shape=[jax.ShapeDtypeStruct(result.shape, result.dtype) for result in results],
        in_specs=[anywhere] * 4,
        out_specs=[anywhere] * 4,
        scratch_shapes=[pltpu.SemaphoreType.DMA((4,))],
        compiler_params=pltpu.CompilerParams(vmem_limit_bytes=1 << 20),
        name="write",
    )(*results)


def solution(mesh):
    in_specs = (
        P("seq", "head"),
        P("seq", "head"),
        P("seq", "head"),
        P("seq", "head"),
        P(),
        P("head"),
        P(),
        P(),
    )
    out_specs = (P("seq", "head"), P("seq", "head"), P("seq", "head"), P("seq", "head", None))
    body = functools.partial(local, mesh.shape["seq"] // X, mesh.shape["head"] // CORES)
    return jax.shard_map(body, mesh=mesh, in_specs=in_specs, out_specs=out_specs, check_vma=False)
```

```python
import functools

import jax
import jax.numpy as jnp
from jax import lax
from jax.experimental import pallas as pl
from jax.experimental.pallas import tpu as pltpu
from jax.sharding import PartitionSpec as P

BLOCK = 256
STATE = 256
HEAD_DIM = 64
HEADS_DEV = 2
X = 4
CORES = 2
PARTS = 4
CHUNKS = 2
MESH = pl.DeviceIdType.MESH
F32 = jnp.float32
BF16 = jnp.bfloat16
NN = (((1,), (0,)), ((), ()))
NT = (((1,), (1,)), ((), ()))
TN = (((0,), (0,)), ((), ()))


def far_first(count):
    return sorted(range(1, count), key=lambda j: -min(j, count - j))


def dot(a, b, dims):
    return lax.dot_general(a, b, dims, preferred_element_type=F32)


def split(a):
    high = a.astype(BF16)
    return high, (a - high.astype(F32)).astype(BF16)


def turn(state, matrix, dims):
    rows = state.shape[0]
    both = dot(jnp.concatenate(split(state), axis=0), matrix, dims)
    return both[:rows] + both[rows:]


def turn_split(state, high, low, dims):
    rows = state.shape[0]
    state_high, state_low = split(state)
    both = dot(jnp.concatenate([state_high, state_low], axis=0), high, dims)
    return both[:rows] + both[rows:] + dot(state_high, low, dims)


def product(a, b):
    a_high, a_low = a
    b_high, b_low = b
    return dot(a_high, b_high, NN) + (dot(a_high, b_low, NN) + dot(a_low, b_high, NN))


def kernel(
    sizes,
    regimes,
    documents,
    gammas,
    q_hbm,
    k_hbm,
    v_hbm,
    g_hbm,
    t_hbm,
    qo,
    ko,
    vo,
    ro,
    q,
    k,
    v,
    g,
    mats,
    q_part,
    k_part,
    v_part,
    update,
    source,
    pairs,
    groups,
    inner,
    t_send,
    t_recv,
    z_send,
    z_pair,
    z_fwd,
    z_bwd,
    s_send,
    s_recv,
    terms,
    h_core,
    h_sum,
    h_y,
    h_block,
    h_x,
    h_reg,
    h_a,
    h_b,
    h_z,
    up_sem,
    down_sem,
    in_sem,
    send_sem,
    recv_sem,
):
    Z, Y, N, HD, B = sizes
    rows = HEADS_DEV * HD
    piece = rows // X
    chunk = piece // CHUNKS
    height = N // (Y * CORES)
    part_rows, width = height // 2, N // 2
    seq = lax.axis_index("seq")
    head = lax.axis_index("head")
    z, x = seq // X, seq % X
    y, core = head // CORES, head % CORES

    def at(dz, dx, dy, dc):
        where = ((z + dz) % Z * X + (x + dx) % X, (y + dy) % Y * CORES + (core + dc) % CORES)
        return where

    loads = [
        pltpu.make_async_copy(src, dst, in_sem.at[i])
        for i, (src, dst) in enumerate(
            [(k_hbm, k), (v_hbm, v), (g_hbm, g), (q_hbm, q), (t_hbm, mats)]
        )
    ]
    for load in loads:
        load.start()

    peers = (
        [at(0, j, 0, 0) for j in range(1, X)]
        + [at(1, 0, 0, 0), at(Z - 1, 0, 0, 0)]
        + [at(0, 0, j, 0) for j in range(1, Y)]
        + [at(0, 0, 0, 1)]
    )
    barrier = pltpu.get_barrier_semaphore()
    for peer in peers:
        pl.semaphore_signal(barrier, inc=1, device_id=peer, device_id_type=MESH)

    used = [0]

    def send(src, dst, peer):
        number = used[0]
        used[0] += 1
        return pltpu.make_async_remote_copy(
            src_ref=src,
            dst_ref=dst,
            send_sem=send_sem.at[number],
            recv_sem=recv_sem.at[number],
            device_id=peer,
            device_id_type=MESH,
        )

    def kept(c):
        same = documents[c] == documents[jnp.maximum(c - 1, 0)]
        return jnp.where(same, 1.0, 0.0).astype(F32) * jnp.where(c > 0, 1.0, 0.0).astype(F32)

    def matrix(c):
        return mats[regimes[c]]

    row_id = lax.broadcasted_iota(jnp.int32, (rows, 1), 0)
    gamma_rows = jnp.where(row_id < HD, gammas[0], gammas[1])
    lane_id = lax.broadcasted_iota(jnp.int32, (1, rows), 1)
    lane_mask = [lane_id < HD, lane_id >= HD]
    first = seq * 2
    keep = [kept(first), kept(first + 1)]

    def tokens(b):
        return slice(b * B, (b + 1) * B)

    def lanes(h):
        return slice(h * N, (h + 1) * N)

    loads[0].wait()
    loads[1].wait()
    for b in range(2):
        flipped = v[tokens(b), :].T
        for h in range(HEADS_DEV):
            part = slice(h * HD, (h + 1) * HD)
            update[b, part, :] = dot(flipped[part], k[tokens(b), lanes(h)], NN)
    loads[2].wait()
    loads[3].wait()
    for b in range(2):
        flipped = g[tokens(b), :].T
        for h in range(HEADS_DEV):
            part = slice(h * HD, (h + 1) * HD)
            source[b, part, :] = dot(flipped[part], q[tokens(b), lanes(h)], NN)
    loads[4].wait()
    m0 = matrix(first)
    m1 = matrix(first + 1)
    ahead = update[1] + keep[1] * gamma_rows * turn(update[0], m1, NT)
    behind = source[0] + keep[1] * gamma_rows * turn(source[1], m1, NN)
    behind = keep[0] * gamma_rows * turn(behind, m0, NN)
    for j in range(X):
        for c in range(CHUNKS):
            part = slice(j * piece + c * chunk, j * piece + (c + 1) * chunk)
            t_send[c, j, 0] = ahead[part]
            t_send[c, j, 1] = behind[part]

    pl.semaphore_wait(barrier, len(peers))
    first_round = [
        [send(t_send.at[c, (x + j) % X], t_recv.at[c, x], at(0, j, 0, 0)) for j in far_first(X)]
        for c in range(CHUNKS)
    ]
    for c in range(CHUNKS):
        for copy in first_round[c]:
            copy.start()
        t_recv[c, x] = t_send[c, x]

    def pass_on():
        pl.semaphore_signal(up_sem, inc=1, device_id=at(1, 0, 0, 0), device_id_type=MESH)
        pl.semaphore_signal(down_sem, inc=1, device_id=at(Z - 1, 0, 0, 0), device_id_type=MESH)

    def hear():
        pl.semaphore_wait(up_sem, 1)
        pl.semaphore_wait(down_sem, 1)

    pass_on()

    def pair_product(c):
        return dot(matrix(c + 1), matrix(c), NN)

    base = z * 2 * X
    for j in range(X):
        high, low = split(pair_product(base + 2 * j))
        pairs[j, 0] = high
        pairs[j, 1] = low

    def pair(j):
        return pairs[j, 0], pairs[j, 1]

    def group_product(offset):
        group = (z + offset + Z) % Z
        made = [split(pair_product(group * 2 * X + 2 * j)) for j in range(X)]
        while len(made) > 1:
            made = [split(product(made[i + 1], made[i])) for i in range(0, len(made), 2)]
        return made[0]

    made = pair(0)
    for j in range(1, X):
        made = split(product(pair(j), made))
        inner[0, j - 1, 0] = made[0]
        inner[0, j - 1, 1] = made[1]
    hear()
    pass_on()

    gamma = gammas[(x * piece) // HD]
    gamma2 = gamma * gamma
    scale = [gamma2 * kept(base + 2 * j) * kept(base + 2 * j + 1) for j in range(X)]

    gamma_group = jnp.float32(1.0)
    for j in range(X):
        gamma_group = gamma_group * gamma2

    def group_scale(offset):
        group = (z + offset + Z) % Z
        total = gamma_group
        for j in range(2 * X):
            total = total * kept(group * 2 * X + j)
        return total

    own = inner[0, X - 2, 0], inner[0, X - 2, 1]
    own_scale = group_scale(0)
    before, after, near, second_round = [], [], [], []
    for c in range(CHUNKS):
        for copy in first_round[c]:
            copy.wait()
        run = t_recv[c, 0, 0]
        run_back = t_recv[c, X - 1, 1]
        fore, back = [None, run], [None] * X
        for j in range(1, X):
            run = t_recv[c, j, 0] + scale[j] * turn_split(run, *pair(j), NT)
            fore.append(run)
            i = X - 1 - j
            back[i] = run_back
            run_back = t_recv[c, i, 1] + scale[i] * turn_split(run_back, *pair(i), NN)
        before.append(fore)
        after.append(back)
        z_send[c, 0] = run
        z_send[c, 1] = run_back
        near.append(
            [
                send(z_send.at[c, 0], z_fwd.at[c, 0], at(1, 0, 0, 0)),
                send(z_send.at[c, 1], z_bwd.at[c, 0], at(Z - 1, 0, 0, 0)),
            ]
        )
        for copy in near[c]:
            copy.start()
    hear()
    for c in range(CHUNKS):
        for copy in near[c]:
            copy.wait()
        z_pair[c, 0] = z_send[c, 0] + own_scale * turn_split(z_fwd[c, 0], *own, NT)
        z_pair[c, 1] = z_send[c, 1] + own_scale * turn_split(z_bwd[c, 0], *own, NN)
        second_round.append(
            [
                send(z_pair.at[c, 0], z_fwd.at[c, 2], at(3, 0, 0, 0)),
                send(z_pair.at[c, 1], z_bwd.at[c, 2], at(Z - 3, 0, 0, 0)),
                send(z_pair.at[c, 0], z_fwd.at[c, 1], at(1, 0, 0, 0)),
                send(z_pair.at[c, 1], z_bwd.at[c, 1], at(Z - 1, 0, 0, 0)),
            ]
        )
        for copy in second_round[c]:
            copy.start()

    made = pair(X - 1)
    for j in reversed(range(1, X - 1)):
        made = split(product(made, pair(j)))
        inner[1, j - 1, 0] = made[0]
        inner[1, j - 1, 1] = made[1]
    back = [group_product(-1), group_product(-2)]
    front = [group_product(1), group_product(2)]
    for i, made in enumerate([product(back[0], back[1]), product(front[1], front[0])]):
        groups[i, 0], groups[i, 1] = split(made)

    back_scale = group_scale(-1) * group_scale(-2)
    front_scale = group_scale(1) * group_scale(2)
    third_round = []
    for c in range(CHUNKS):
        for copy in second_round[c]:
            copy.wait()
        inbound = z_fwd[c, 1] + back_scale * turn_split(
            z_fwd[c, 2], groups[0, 0], groups[0, 1], NT
        )
        outbound = z_bwd[c, 1] + front_scale * turn_split(
            z_bwd[c, 2], groups[1, 0], groups[1, 1], NN
        )
        s_send[c, 0, 0] = inbound
        total_scale = scale[0]
        for j in range(1, X):
            made = pair(0) if j == 1 else (inner[0, j - 2, 0], inner[0, j - 2, 1])
            s_send[c, j, 0] = before[c][j] + total_scale * turn_split(inbound, *made, NT)
            total_scale = total_scale * scale[j]
        s_send[c, X - 1, 1] = outbound
        total_scale = scale[X - 1]
        for j in reversed(range(X - 1)):
            made = pair(X - 1) if j == X - 2 else (inner[1, j, 0], inner[1, j, 1])
            s_send[c, j, 1] = after[c][j] + total_scale * turn_split(outbound, *made, NN)
            total_scale = total_scale * scale[j]
        third_round.append(
            [send(s_send.at[c, (x + j) % X], s_recv.at[c, x], at(0, j, 0, 0)) for j in far_first(X)]
        )
        for copy in third_round[c]:
            copy.start()
        s_recv[c, x] = s_send[c, x]

    row = lax.broadcasted_iota(jnp.int32, (B, B), 0)
    column = lax.broadcasted_iota(jnp.int32, (B, B), 1)
    for b in range(2):
        for h in range(HEADS_DEV):
            q_block = q[tokens(b), lanes(h)]
            k_block = k[tokens(b), lanes(h)]
            v_block = v[tokens(b), :]
            g_block = g[tokens(b), :]
            zero = jnp.zeros_like(g_block)
            g_head = jnp.where(lane_mask[h], g_block, zero)
            probs = jnp.where(row <= column, dot(k_block, q_block, NT), 0.0).astype(BF16)
            scored = jnp.where(row >= column, dot(g_head, v_block, NT), 0.0).astype(BF16)
            turned = jnp.where(row <= column, dot(v_block, g_head, NT), 0.0).astype(BF16)
            q_part[tokens(b), lanes(h)] = dot(scored, k_block, NN)
            k_part[tokens(b), lanes(h)] = dot(turned, q_block, NN)
            if h == 0:
                v_part[tokens(b), :] = dot(probs, g_head, NN)
            else:
                v_part[tokens(b), :] += dot(probs, g_head, NN)

    for copies in third_round:
        for copy in copies:
            copy.wait()

    order = [(c, j) for j in range(X) for c in range(CHUNKS)]
    previous = jnp.concatenate([s_recv[c, j, 0] for c, j in order], axis=0)
    leaving = jnp.concatenate([s_recv[c, j, 1] for c, j in order], axis=0)
    total1 = source[1] + leaving
    entry0 = keep[0] * gamma_rows * turn(previous, m0, NT)
    leave0 = keep[1] * gamma_rows * turn(total1, m1, NN)
    end0 = entry0 + update[0]
    total0 = source[0] + leave0
    for b, (outer, inside) in enumerate([(total0, previous), (total1, end0)]):
        left_high, left_low = split(outer * (keep[b] * gamma_rows))
        right_high, right_low = split(inside)
        term = dot(
            jnp.concatenate([left_high, left_low, left_high], axis=0),
            jnp.concatenate([right_high, right_high, right_low], axis=0),
            TN,
        )
        for j in range(Y * CORES):
            for t in range(PARTS):
                top, left = j * height + t % 2 * part_rows, t // 2 * width
                terms[t, j % CORES, j // CORES, b] = term[
                    top : top + part_rows, left : left + width
                ]
    core_round = [send(terms.at[t, 1 - core], h_core.at[t], at(0, 0, 0, 1)) for t in range(PARTS)]
    for copy in core_round:
        copy.start()

    entry1 = keep[1] * gamma_rows * turn(end0, m1, NT)
    entries = [entry0.astype(BF16), entry1.astype(BF16)]
    leaves = [leave0.astype(BF16), leaving.astype(BF16)]

    y_round = []
    for t in range(PARTS):
        core_round[t].wait()
        for j in range(Y):
            h_sum[t, j] = terms[t, core, j] + h_core[t, j]
        copies = [
            send(h_sum.at[t, (y + j) % Y], h_y.at[t, j - 1], at(0, 0, j, 0)) for j in far_first(Y)
        ]
        for copy in copies:
            copy.start()
        y_round.append(copies)
    x_round = []
    for t in range(PARTS):
        for copy in y_round[t]:
            copy.wait()
        mine = h_sum[t, y]
        for j in range(Y - 1):
            mine = mine + h_y[t, j]
        h_block[t] = mine
        copies = [send(h_block.at[t], h_x.at[t, x], at(0, j, 0, 0)) for j in far_first(X)]
        for copy in copies:
            copy.start()
        x_round.append(copies)
        h_x[t, x] = mine
    chosen = [
        [
            jnp.where(regimes[base + i] == (z + j) % Z * X + x, 1.0, 0.0).astype(F32)
            for i in range(2 * X)
        ]
        for j in range(Z)
    ]
    a_round = []
    z_round = []
    for t in range(PARTS):
        for copy in x_round[t]:
            copy.wait()
        for j in range(Z):
            total = chosen[j][0] * h_x[t, 0, 0]
            for i in range(1, 2 * X):
                total = total + chosen[j][i] * h_x[t, i // 2, i % 2]
            h_reg[t, j] = total
        half = 2 if t % 2 == 0 else Z - 2
        first_leg = [
            send(h_reg.at[t, 4], h_a.at[t, 0], at(half, 0, 0, 0)),
            send(h_reg.at[t, 3], h_a.at[t, 1], at(1, 0, 0, 0)),
            send(h_reg.at[t, Z - 3], h_a.at[t, 2], at(Z - 1, 0, 0, 0)),
        ]
        next_leg = [
            send(h_reg.at[t, 1], h_z.at[t, 0], at(1, 0, 0, 0)),
            send(h_reg.at[t, Z - 1], h_z.at[t, 1], at(Z - 1, 0, 0, 0)),
        ]
        for copy in first_leg + next_leg:
            copy.start()
        a_round.append(first_leg)
        z_round.append(next_leg)
    for t in range(PARTS):
        for copy in a_round[t]:
            copy.wait()
        ahead2 = h_reg[t, 2] + h_a[t, 1]
        behind2 = h_reg[t, Z - 2] + h_a[t, 2]
        if t % 2 == 0:
            ahead2 = ahead2 + h_a[t, 0]
        else:
            behind2 = behind2 + h_a[t, 0]
        h_b[t, 0] = ahead2
        h_b[t, 1] = behind2
        copies = [
            send(h_b.at[t, 0], h_z.at[t, 2], at(2, 0, 0, 0)),
            send(h_b.at[t, 1], h_z.at[t, 3], at(Z - 2, 0, 0, 0)),
        ]
        for copy in copies:
            copy.start()
        z_round[t] += copies

    for b in range(2):
        v_block = v[tokens(b), :]
        g_block = g[tokens(b), :]
        zero = jnp.zeros_like(g_block)
        v_new = v_part[tokens(b), :]
        for h in range(HEADS_DEV):
            g_head = jnp.where(lane_mask[h], g_block, zero)
            v_head = jnp.where(lane_mask[h], v_block, zero)
            qo[tokens(b), lanes(h)] = (
                q_part[tokens(b), lanes(h)] + dot(g_head, entries[b], NN)
            ).astype(BF16)
            ko[tokens(b), lanes(h)] = (
                k_part[tokens(b), lanes(h)] + dot(v_head, leaves[b], NN)
            ).astype(BF16)
            v_new = v_new + jnp.where(
                lane_mask[h], dot(k[tokens(b), lanes(h)], leaves[b], NT), 0.0
            )
        vo[tokens(b), :] = v_new.astype(BF16)

    for t in range(PARTS):
        for copy in z_round[t]:
            copy.wait()
        total = h_reg[t, 0]
        for j in range(4):
            total = total + h_z[t, j]
        top, left = t % 2 * part_rows, t // 2 * width
        ro[0, top : top + part_rows, left : left + width] = total


def write(*refs):
    count = (len(refs) - 1) // 2
    sem = refs[-1]
    copies = [pltpu.make_async_copy(refs[i], refs[count + i], sem.at[i]) for i in range(count)]
    for copy in copies:
        copy.start()
    for copy in copies:
        copy.wait()


def local(Z, Y, queries, keys, values, out_grad, transitions, gammas, regimes, documents):
    tokens_dev = queries.shape[0]
    N = transitions.shape[1]
    rows = values.shape[1]
    HD = rows // HEADS_DEV
    B = tokens_dev // 2
    chunk = rows // X // CHUNKS
    height = N // (Y * CORES)
    anywhere = pl.BlockSpec(memory_space=pl.ANY)
    scalar = pl.BlockSpec(memory_space=pltpu.SMEM)
    vmem = pltpu.VMEM
    part_rows, width = height // 2, N // 2
    copies = CHUNKS * (2 * (X - 1) + 6) + PARTS * (1 + (Y - 1) + (X - 1) + 7)
    results = pl.pallas_call(
        functools.partial(kernel, (Z, Y, N, HD, B)),
        out_shape=(
            vmem(queries.shape, BF16),
            vmem(keys.shape, BF16),
            vmem(values.shape, BF16),
            vmem((1, height, N), F32),
        ),
        in_specs=[scalar] * 3 + [anywhere] * 5,
        out_specs=[pl.BlockSpec(memory_space=vmem)] * 4,
        scratch_shapes=[
            vmem(queries.shape, BF16),
            vmem(keys.shape, BF16),
            vmem(values.shape, BF16),
            vmem(values.shape, BF16),
            vmem(transitions.shape, BF16),
            vmem(queries.shape, F32),
            vmem(keys.shape, F32),
            vmem(values.shape, F32),
            vmem((2, rows, N), F32),
            vmem((2, rows, N), F32),
            vmem((X, 2, N, N), BF16),
            vmem((2, 2, N, N), BF16),
            vmem((2, X - 1, 2, N, N), BF16),
            vmem((CHUNKS, X, 2, chunk, N), F32),
            vmem((CHUNKS, X, 2, chunk, N), F32),
            vmem((CHUNKS, 2, chunk, N), F32),
            vmem((CHUNKS, 2, chunk, N), F32),
            vmem((CHUNKS, 3, chunk, N), F32),
            vmem((CHUNKS, 3, chunk, N), F32),
            vmem((CHUNKS, X, 2, chunk, N), F32),
            vmem((CHUNKS, X, 2, chunk, N), F32),
            vmem((PARTS, CORES, Y, 2, part_rows, width), F32),
            vmem((PARTS, Y, 2, part_rows, width), F32),
            vmem((PARTS, Y, 2, part_rows, width), F32),
            vmem((PARTS, Y - 1, 2, part_rows, width), F32),
            vmem((PARTS, 2, part_rows, width), F32),
            vmem((PARTS, X, 2, part_rows, width), F32),
            vmem((PARTS, Z, part_rows, width), F32),
            vmem((PARTS, 3, part_rows, width), F32),
            vmem((PARTS, 2, part_rows, width), F32),
            vmem((PARTS, 4, part_rows, width), F32),
            pltpu.SemaphoreType.REGULAR,
            pltpu.SemaphoreType.REGULAR,
            pltpu.SemaphoreType.DMA((5,)),
            pltpu.SemaphoreType.DMA((copies,)),
            pltpu.SemaphoreType.DMA((copies,)),
        ],
        compiler_params=pltpu.CompilerParams(collective_id=0, has_side_effects=True),
        name="whole",
    )(regimes, documents, gammas, queries, keys, values, out_grad, transitions)
    return pl.pallas_call(
        write,
        out_shape=[jax.ShapeDtypeStruct(result.shape, result.dtype) for result in results],
        in_specs=[anywhere] * 4,
        out_specs=[anywhere] * 4,
        scratch_shapes=[pltpu.SemaphoreType.DMA((4,))],
        compiler_params=pltpu.CompilerParams(vmem_limit_bytes=1 << 20),
        name="write",
    )(*results)


def solution(mesh):
    in_specs = (
        P("seq", "head"),
        P("seq", "head"),
        P("seq", "head"),
        P("seq", "head"),
        P(),
        P("head"),
        P(),
        P(),
    )
    out_specs = (P("seq", "head"), P("seq", "head"), P("seq", "head"), P("seq", "head", None))
    body = functools.partial(local, mesh.shape["seq"] // X, mesh.shape["head"] // CORES)
    return jax.shard_map(body, mesh=mesh, in_specs=in_specs, out_specs=out_specs, check_vma=False)
```

```python
import functools

import jax
import jax.numpy as jnp
from jax import lax
from jax.experimental import pallas as pl
from jax.experimental.pallas import tpu as pltpu
from jax.sharding import PartitionSpec as P

BLOCK = 256
STATE = 256
HEAD_DIM = 64
HEADS_DEV = 2
X = 4
CORES = 2
PARTS = 4
CHUNKS = 2
MESH = pl.DeviceIdType.MESH
F32 = jnp.float32
BF16 = jnp.bfloat16
NN = (((1,), (0,)), ((), ()))
NT = (((1,), (1,)), ((), ()))
TN = (((0,), (0,)), ((), ()))


def far_first(count):
    return sorted(range(1, count), key=lambda j: -min(j, count - j))


def dot(a, b, dims):
    return lax.dot_general(a, b, dims, preferred_element_type=F32)


def split(a):
    high = a.astype(BF16)
    return high, (a - high.astype(F32)).astype(BF16)


def turn(state, matrix, dims):
    rows = state.shape[0]
    both = dot(jnp.concatenate(split(state), axis=0), matrix, dims)
    return both[:rows] + both[rows:]


def turn_split(state, high, low, dims):
    rows = state.shape[0]
    state_high, state_low = split(state)
    both = dot(jnp.concatenate([state_high, state_low], axis=0), high, dims)
    return both[:rows] + both[rows:] + dot(state_high, low, dims)


def product(a, b):
    a_high, a_low = a
    b_high, b_low = b
    return dot(a_high, b_high, NN) + (dot(a_high, b_low, NN) + dot(a_low, b_high, NN))


def kernel(
    sizes,
    regimes_hbm,
    documents_hbm,
    gammas_hbm,
    q_hbm,
    k_hbm,
    v_hbm,
    g_hbm,
    t_hbm,
    qo,
    ko,
    vo,
    ro,
    regimes,
    documents,
    gammas,
    q,
    k,
    v,
    g,
    mats,
    q_part,
    k_part,
    v_part,
    update,
    source,
    pairs,
    groups,
    inner,
    t_send,
    t_recv,
    z_send,
    z_pair,
    z_fwd,
    z_bwd,
    s_send,
    s_recv,
    terms,
    h_core,
    h_sum,
    h_y,
    h_block,
    h_x,
    h_reg,
    h_z,
    up_sem,
    down_sem,
    in_sem,
    send_sem,
    recv_sem,
):
    Z, Y, N, HD, B = sizes
    rows = HEADS_DEV * HD
    piece = rows // X
    chunk = piece // CHUNKS
    height = N // (Y * CORES)
    part_rows, width = height // 2, N // 2
    seq = lax.axis_index("seq")
    head = lax.axis_index("head")
    z, x = seq // X, seq % X
    y, core = head // CORES, head % CORES

    def at(dz, dx, dy, dc):
        where = ((z + dz) % Z * X + (x + dx) % X, (y + dy) % Y * CORES + (core + dc) % CORES)
        return where

    loads = [
        pltpu.make_async_copy(src, dst, in_sem.at[i])
        for i, (src, dst) in enumerate(
            [
                (k_hbm, k),
                (v_hbm, v),
                (g_hbm, g),
                (q_hbm, q),
                (t_hbm, mats),
                (gammas_hbm, gammas),
                (regimes_hbm, regimes),
                (documents_hbm, documents),
            ]
        )
    ]
    for load in loads:
        load.start()

    peers = (
        [at(0, j, 0, 0) for j in range(1, X)]
        + [at(1, 0, 0, 0), at(Z - 1, 0, 0, 0)]
        + [at(0, 0, j, 0) for j in range(1, Y)]
        + [at(0, 0, 0, 1)]
    )
    barrier = pltpu.get_barrier_semaphore()
    for peer in peers:
        pl.semaphore_signal(barrier, inc=1, device_id=peer, device_id_type=MESH)

    used = [0]

    def send(src, dst, peer):
        number = used[0]
        used[0] += 1
        return pltpu.make_async_remote_copy(
            src_ref=src,
            dst_ref=dst,
            send_sem=send_sem.at[number],
            recv_sem=recv_sem.at[number],
            device_id=peer,
            device_id_type=MESH,
        )

    def kept(c):
        same = documents[c] == documents[jnp.maximum(c - 1, 0)]
        return jnp.where(same, 1.0, 0.0).astype(F32) * jnp.where(c > 0, 1.0, 0.0).astype(F32)

    def matrix(c):
        return mats[regimes[c]]

    lane_id = lax.broadcasted_iota(jnp.int32, (1, rows), 1)
    lane_mask = [lane_id < HD, lane_id >= HD]
    first = seq * 2

    def tokens(b):
        return slice(b * B, (b + 1) * B)

    def lanes(h):
        return slice(h * N, (h + 1) * N)

    loads[0].wait()
    loads[1].wait()
    for b in range(2):
        flipped = v[tokens(b), :].T
        for h in range(HEADS_DEV):
            part = slice(h * HD, (h + 1) * HD)
            update[b, part, :] = dot(flipped[part], k[tokens(b), lanes(h)], NN)
    loads[2].wait()
    loads[3].wait()
    for b in range(2):
        flipped = g[tokens(b), :].T
        for h in range(HEADS_DEV):
            part = slice(h * HD, (h + 1) * HD)
            source[b, part, :] = dot(flipped[part], q[tokens(b), lanes(h)], NN)
    for load in loads[4:]:
        load.wait()
    row_id = lax.broadcasted_iota(jnp.int32, (rows, 1), 0)
    gamma_rows = jnp.where(row_id < HD, gammas[0], gammas[1])
    keep = [kept(first), kept(first + 1)]
    m0 = matrix(first)
    m1 = matrix(first + 1)
    ahead = update[1] + keep[1] * gamma_rows * turn(update[0], m1, NT)
    behind = source[0] + keep[1] * gamma_rows * turn(source[1], m1, NN)
    behind = keep[0] * gamma_rows * turn(behind, m0, NN)
    for j in range(X):
        for c in range(CHUNKS):
            part = slice(j * piece + c * chunk, j * piece + (c + 1) * chunk)
            t_send[c, j, 0] = ahead[part]
            t_send[c, j, 1] = behind[part]

    pl.semaphore_wait(barrier, len(peers))
    first_round = [
        [send(t_send.at[c, (x + j) % X], t_recv.at[c, x], at(0, j, 0, 0)) for j in far_first(X)]
        for c in range(CHUNKS)
    ]
    for c in range(CHUNKS):
        for copy in first_round[c]:
            copy.start()
        t_recv[c, x] = t_send[c, x]

    def pass_on():
        pl.semaphore_signal(up_sem, inc=1, device_id=at(1, 0, 0, 0), device_id_type=MESH)
        pl.semaphore_signal(down_sem, inc=1, device_id=at(Z - 1, 0, 0, 0), device_id_type=MESH)

    def hear():
        pl.semaphore_wait(up_sem, 1)
        pl.semaphore_wait(down_sem, 1)

    pass_on()

    def pair_product(c):
        return dot(matrix(c + 1), matrix(c), NN)

    base = z * 2 * X
    for j in range(X):
        high, low = split(pair_product(base + 2 * j))
        pairs[j, 0] = high
        pairs[j, 1] = low

    def pair(j):
        return pairs[j, 0], pairs[j, 1]

    def group_product(offset):
        group = (z + offset + Z) % Z
        made = [split(pair_product(group * 2 * X + 2 * j)) for j in range(X)]
        while len(made) > 1:
            made = [split(product(made[i + 1], made[i])) for i in range(0, len(made), 2)]
        return made[0]

    made = pair(0)
    for j in range(1, X):
        made = split(product(pair(j), made))
        inner[0, j - 1, 0] = made[0]
        inner[0, j - 1, 1] = made[1]
    hear()
    pass_on()

    gamma = gammas[(x * piece) // HD]
    gamma2 = gamma * gamma
    scale = [gamma2 * kept(base + 2 * j) * kept(base + 2 * j + 1) for j in range(X)]

    gamma_group = jnp.float32(1.0)
    for j in range(X):
        gamma_group = gamma_group * gamma2

    def group_scale(offset):
        group = (z + offset + Z) % Z
        total = gamma_group
        for j in range(2 * X):
            total = total * kept(group * 2 * X + j)
        return total

    own = inner[0, X - 2, 0], inner[0, X - 2, 1]
    own_scale = group_scale(0)
    before, after, near, second_round = [], [], [], []
    for c in range(CHUNKS):
        for copy in first_round[c]:
            copy.wait()
        run = t_recv[c, 0, 0]
        run_back = t_recv[c, X - 1, 1]
        fore, back = [None, run], [None] * X
        for j in range(1, X):
            run = t_recv[c, j, 0] + scale[j] * turn_split(run, *pair(j), NT)
            fore.append(run)
            i = X - 1 - j
            back[i] = run_back
            run_back = t_recv[c, i, 1] + scale[i] * turn_split(run_back, *pair(i), NN)
        before.append(fore)
        after.append(back)
        z_send[c, 0] = run
        z_send[c, 1] = run_back
        near.append(
            [
                send(z_send.at[c, 0], z_fwd.at[c, 0], at(1, 0, 0, 0)),
                send(z_send.at[c, 1], z_bwd.at[c, 0], at(Z - 1, 0, 0, 0)),
            ]
        )
        for copy in near[c]:
            copy.start()
    hear()
    pass_on()
    for c in range(CHUNKS):
        for copy in near[c]:
            copy.wait()
        z_pair[c, 0] = z_send[c, 0] + own_scale * turn_split(z_fwd[c, 0], *own, NT)
        z_pair[c, 1] = z_send[c, 1] + own_scale * turn_split(z_bwd[c, 0], *own, NN)
        second_round.append(
            [
                send(z_pair.at[c, 0], z_fwd.at[c, 2], at(3, 0, 0, 0)),
                send(z_pair.at[c, 1], z_bwd.at[c, 2], at(Z - 3, 0, 0, 0)),
                send(z_pair.at[c, 0], z_fwd.at[c, 1], at(1, 0, 0, 0)),
                send(z_pair.at[c, 1], z_bwd.at[c, 1], at(Z - 1, 0, 0, 0)),
            ]
        )
        for copy in second_round[c]:
            copy.start()

    made = pair(X - 1)
    for j in reversed(range(1, X - 1)):
        made = split(product(made, pair(j)))
        inner[1, j - 1, 0] = made[0]
        inner[1, j - 1, 1] = made[1]
    back = [group_product(-1), group_product(-2)]
    front = [group_product(1), group_product(2)]
    for i, made in enumerate([product(back[0], back[1]), product(front[1], front[0])]):
        groups[i, 0], groups[i, 1] = split(made)

    back_scale = group_scale(-1) * group_scale(-2)
    front_scale = group_scale(1) * group_scale(2)
    third_round = []
    for c in range(CHUNKS):
        for copy in second_round[c]:
            copy.wait()
        inbound = z_fwd[c, 1] + back_scale * turn_split(
            z_fwd[c, 2], groups[0, 0], groups[0, 1], NT
        )
        outbound = z_bwd[c, 1] + front_scale * turn_split(
            z_bwd[c, 2], groups[1, 0], groups[1, 1], NN
        )
        s_send[c, 0, 0] = inbound
        total_scale = scale[0]
        for j in range(1, X):
            made = pair(0) if j == 1 else (inner[0, j - 2, 0], inner[0, j - 2, 1])
            s_send[c, j, 0] = before[c][j] + total_scale * turn_split(inbound, *made, NT)
            total_scale = total_scale * scale[j]
        s_send[c, X - 1, 1] = outbound
        total_scale = scale[X - 1]
        for j in reversed(range(X - 1)):
            made = pair(X - 1) if j == X - 2 else (inner[1, j, 0], inner[1, j, 1])
            s_send[c, j, 1] = after[c][j] + total_scale * turn_split(outbound, *made, NN)
            total_scale = total_scale * scale[j]
        third_round.append(
            [send(s_send.at[c, (x + j) % X], s_recv.at[c, x], at(0, j, 0, 0)) for j in far_first(X)]
        )
        for copy in third_round[c]:
            copy.start()
        s_recv[c, x] = s_send[c, x]

    row = lax.broadcasted_iota(jnp.int32, (B, B), 0)
    column = lax.broadcasted_iota(jnp.int32, (B, B), 1)
    for b in range(2):
        for h in range(HEADS_DEV):
            q_block = q[tokens(b), lanes(h)]
            k_block = k[tokens(b), lanes(h)]
            v_block = v[tokens(b), :]
            g_block = g[tokens(b), :]
            zero = jnp.zeros_like(g_block)
            g_head = jnp.where(lane_mask[h], g_block, zero)
            probs = jnp.where(row <= column, dot(k_block, q_block, NT), 0.0).astype(BF16)
            scored = jnp.where(row >= column, dot(g_head, v_block, NT), 0.0).astype(BF16)
            turned = jnp.where(row <= column, dot(v_block, g_head, NT), 0.0).astype(BF16)
            q_part[tokens(b), lanes(h)] = dot(scored, k_block, NN)
            k_part[tokens(b), lanes(h)] = dot(turned, q_block, NN)
            if h == 0:
                v_part[tokens(b), :] = dot(probs, g_head, NN)
            else:
                v_part[tokens(b), :] += dot(probs, g_head, NN)

    for copies in third_round:
        for copy in copies:
            copy.wait()

    order = [(c, j) for j in range(X) for c in range(CHUNKS)]
    previous = jnp.concatenate([s_recv[c, j, 0] for c, j in order], axis=0)
    leaving = jnp.concatenate([s_recv[c, j, 1] for c, j in order], axis=0)
    total1 = source[1] + leaving
    entry0 = keep[0] * gamma_rows * turn(previous, m0, NT)
    leave0 = keep[1] * gamma_rows * turn(total1, m1, NN)
    end0 = entry0 + update[0]
    total0 = source[0] + leave0
    for b, (outer, inside) in enumerate([(total0, previous), (total1, end0)]):
        left_high, left_low = split(outer * (keep[b] * gamma_rows))
        right_high, right_low = split(inside)
        term = dot(
            jnp.concatenate([left_high, left_low, left_high], axis=0),
            jnp.concatenate([right_high, right_high, right_low], axis=0),
            TN,
        )
        for j in range(Y * CORES):
            for t in range(PARTS):
                top, left = j * height + t % 2 * part_rows, t // 2 * width
                terms[t, j % CORES, j // CORES, b] = term[
                    top : top + part_rows, left : left + width
                ]
    core_round = [send(terms.at[t, 1 - core], h_core.at[t], at(0, 0, 0, 1)) for t in range(PARTS)]
    for copy in core_round:
        copy.start()

    entry1 = keep[1] * gamma_rows * turn(end0, m1, NT)
    entries = [entry0.astype(BF16), entry1.astype(BF16)]
    leaves = [leave0.astype(BF16), leaving.astype(BF16)]

    y_round = []
    for t in range(PARTS):
        core_round[t].wait()
        for j in range(Y):
            h_sum[t, j] = terms[t, core, j] + h_core[t, j]
        copies = [
            send(h_sum.at[t, (y + j) % Y], h_y.at[t, j - 1], at(0, 0, j, 0)) for j in far_first(Y)
        ]
        for copy in copies:
            copy.start()
        y_round.append(copies)
    x_round = []
    for t in range(PARTS):
        for copy in y_round[t]:
            copy.wait()
        mine = h_sum[t, y]
        for j in range(Y - 1):
            mine = mine + h_y[t, j]
        h_block[t] = mine
        copies = [send(h_block.at[t], h_x.at[t, x], at(0, j, 0, 0)) for j in far_first(X)]
        for copy in copies:
            copy.start()
        x_round.append(copies)
        h_x[t, x] = mine
    chosen = [
        [
            jnp.where(regimes[base + i] == (z + j) % Z * X + x, 1.0, 0.0).astype(F32)
            for i in range(2 * X)
        ]
        for j in range(Z)
    ]
    hear()
    z_round = []
    for t in range(PARTS):
        for copy in x_round[t]:
            copy.wait()
        for j in range(Z):
            total = chosen[j][0] * h_x[t, 0, 0]
            for i in range(1, 2 * X):
                total = total + chosen[j][i] * h_x[t, i // 2, i % 2]
            h_reg[t, j] = total
        copies = [
            send(h_reg.at[t, j], h_z.at[t, j - 1], at(j, 0, 0, 0)) for j in far_first(Z)
        ]
        for copy in copies:
            copy.start()
        z_round.append(copies)

    for b in range(2):
        v_block = v[tokens(b), :]
        g_block = g[tokens(b), :]
        zero = jnp.zeros_like(g_block)
        v_new = v_part[tokens(b), :]
        for h in range(HEADS_DEV):
            g_head = jnp.where(lane_mask[h], g_block, zero)
            v_head = jnp.where(lane_mask[h], v_block, zero)
            qo[tokens(b), lanes(h)] = (
                q_part[tokens(b), lanes(h)] + dot(g_head, entries[b], NN)
            ).astype(BF16)
            ko[tokens(b), lanes(h)] = (
                k_part[tokens(b), lanes(h)] + dot(v_head, leaves[b], NN)
            ).astype(BF16)
            v_new = v_new + jnp.where(
                lane_mask[h], dot(k[tokens(b), lanes(h)], leaves[b], NT), 0.0
            )
        vo[tokens(b), :] = v_new.astype(BF16)

    for t in range(PARTS):
        for copy in z_round[t]:
            copy.wait()
        total = h_reg[t, 0]
        for j in range(Z - 1):
            total = total + h_z[t, j]
        top, left = t % 2 * part_rows, t // 2 * width
        ro[0, top : top + part_rows, left : left + width] = total


def write(*refs):
    count = (len(refs) - 1) // 2
    sem = refs[-1]
    copies = [pltpu.make_async_copy(refs[i], refs[count + i], sem.at[i]) for i in range(count)]
    for copy in copies:
        copy.start()
    for copy in copies:
        copy.wait()


def local(Z, Y, queries, keys, values, out_grad, transitions, gammas, regimes, documents):
    tokens_dev = queries.shape[0]
    N = transitions.shape[1]
    rows = values.shape[1]
    HD = rows // HEADS_DEV
    B = tokens_dev // 2
    chunk = rows // X // CHUNKS
    height = N // (Y * CORES)
    anywhere = pl.BlockSpec(memory_space=pl.ANY)
    vmem = pltpu.VMEM
    part_rows, width = height // 2, N // 2
    copies = CHUNKS * (2 * (X - 1) + 6) + PARTS * (1 + (Y - 1) + (X - 1) + 7)
    results = pl.pallas_call(
        functools.partial(kernel, (Z, Y, N, HD, B)),
        out_shape=(
            vmem(queries.shape, BF16),
            vmem(keys.shape, BF16),
            vmem(values.shape, BF16),
            vmem((1, height, N), F32),
        ),
        in_specs=[anywhere] * 8,
        out_specs=[pl.BlockSpec(memory_space=vmem)] * 4,
        scratch_shapes=[
            pltpu.SMEM(regimes.shape, jnp.int32),
            pltpu.SMEM(documents.shape, jnp.int32),
            pltpu.SMEM(gammas.shape, F32),
            vmem(queries.shape, BF16),
            vmem(keys.shape, BF16),
            vmem(values.shape, BF16),
            vmem(values.shape, BF16),
            vmem(transitions.shape, BF16),
            vmem(queries.shape, F32),
            vmem(keys.shape, F32),
            vmem(values.shape, F32),
            vmem((2, rows, N), F32),
            vmem((2, rows, N), F32),
            vmem((X, 2, N, N), BF16),
            vmem((2, 2, N, N), BF16),
            vmem((2, X - 1, 2, N, N), BF16),
            vmem((CHUNKS, X, 2, chunk, N), F32),
            vmem((CHUNKS, X, 2, chunk, N), F32),
            vmem((CHUNKS, 2, chunk, N), F32),
            vmem((CHUNKS, 2, chunk, N), F32),
            vmem((CHUNKS, 3, chunk, N), F32),
            vmem((CHUNKS, 3, chunk, N), F32),
            vmem((CHUNKS, X, 2, chunk, N), F32),
            vmem((CHUNKS, X, 2, chunk, N), F32),
            vmem((PARTS, CORES, Y, 2, part_rows, width), F32),
            vmem((PARTS, Y, 2, part_rows, width), F32),
            vmem((PARTS, Y, 2, part_rows, width), F32),
            vmem((PARTS, Y - 1, 2, part_rows, width), F32),
            vmem((PARTS, 2, part_rows, width), F32),
            vmem((PARTS, X, 2, part_rows, width), F32),
            vmem((PARTS, Z, part_rows, width), F32),
            vmem((PARTS, Z - 1, part_rows, width), F32),
            pltpu.SemaphoreType.REGULAR,
            pltpu.SemaphoreType.REGULAR,
            pltpu.SemaphoreType.DMA((8,)),
            pltpu.SemaphoreType.DMA((copies,)),
            pltpu.SemaphoreType.DMA((copies,)),
        ],
        compiler_params=pltpu.CompilerParams(collective_id=0, has_side_effects=True),
        name="whole",
    )(regimes, documents, gammas, queries, keys, values, out_grad, transitions)
    return pl.pallas_call(
        write,
        out_shape=[jax.ShapeDtypeStruct(result.shape, result.dtype) for result in results],
        in_specs=[anywhere] * 4,
        out_specs=[anywhere] * 4,
        scratch_shapes=[pltpu.SemaphoreType.DMA((4,))],
        compiler_params=pltpu.CompilerParams(vmem_limit_bytes=1 << 20),
        name="write",
    )(*results)


def solution(mesh):
    in_specs = (
        P("seq", "head"),
        P("seq", "head"),
        P("seq", "head"),
        P("seq", "head"),
        P(),
        P("head"),
        P(),
        P(),
    )
    out_specs = (P("seq", "head"), P("seq", "head"), P("seq", "head"), P("seq", "head", None))
    body = functools.partial(local, mesh.shape["seq"] // X, mesh.shape["head"] // CORES)
    return jax.shard_map(body, mesh=mesh, in_specs=in_specs, out_specs=out_specs, check_vma=False)
```

```python
import functools

import jax
import jax.numpy as jnp
from jax import lax
from jax.experimental import pallas as pl
from jax.experimental.pallas import tpu as pltpu
from jax.sharding import PartitionSpec as P

BLOCK = 256
STATE = 256
HEAD_DIM = 64
HEADS_DEV = 2
X = 4
CORES = 2
PARTS = 4
CHUNKS = 2
MESH = pl.DeviceIdType.MESH
F32 = jnp.float32
BF16 = jnp.bfloat16
NN = (((1,), (0,)), ((), ()))
NT = (((1,), (1,)), ((), ()))
TN = (((0,), (0,)), ((), ()))


def far_first(count):
    return sorted(range(1, count), key=lambda j: -min(j, count - j))


def dot(a, b, dims):
    return lax.dot_general(a, b, dims, preferred_element_type=F32)


def split(a):
    high = a.astype(BF16)
    return high, (a - high.astype(F32)).astype(BF16)


def turn(state, matrix, dims):
    rows = state.shape[0]
    both = dot(jnp.concatenate(split(state), axis=0), matrix, dims)
    return both[:rows] + both[rows:]


def turn_split(state, high, low, dims):
    rows = state.shape[0]
    state_high, state_low = split(state)
    both = dot(jnp.concatenate([state_high, state_low], axis=0), high, dims)
    return both[:rows] + both[rows:] + dot(state_high, low, dims)


def product(a, b):
    a_high, a_low = a
    b_high, b_low = b
    return dot(a_high, b_high, NN) + (dot(a_high, b_low, NN) + dot(a_low, b_high, NN))


def kernel(
    sizes,
    regimes_hbm,
    documents_hbm,
    gammas_hbm,
    q_hbm,
    k_hbm,
    v_hbm,
    g_hbm,
    t_hbm,
    qo,
    ko,
    vo,
    ro,
    regimes,
    documents,
    gammas,
    q,
    k,
    v,
    g,
    mats,
    q_part,
    k_part,
    v_part,
    update,
    source,
    pairs,
    groups,
    inner,
    t_send,
    t_recv,
    z_send,
    z_pair,
    z_fwd,
    z_bwd,
    s_send,
    s_recv,
    terms,
    h_core,
    h_sum,
    h_y,
    h_block,
    h_x,
    h_reg,
    h_z,
    up_sem,
    down_sem,
    in_sem,
    send_sem,
    recv_sem,
):
    Z, Y, N, HD, B = sizes
    rows = HEADS_DEV * HD
    piece = rows // X
    chunk = piece // CHUNKS
    height = N // (Y * CORES)
    part_rows, width = height // 2, N // 2
    seq = lax.axis_index("seq")
    head = lax.axis_index("head")
    z, x = seq // X, seq % X
    y, core = head // CORES, head % CORES

    def at(dz, dx, dy, dc):
        where = ((z + dz) % Z * X + (x + dx) % X, (y + dy) % Y * CORES + (core + dc) % CORES)
        return where

    loads = [
        pltpu.make_async_copy(src, dst, in_sem.at[i])
        for i, (src, dst) in enumerate(
            [
                (k_hbm, k),
                (v_hbm, v),
                (g_hbm, g),
                (q_hbm, q),
                (t_hbm, mats),
                (gammas_hbm, gammas),
                (regimes_hbm, regimes),
                (documents_hbm, documents),
            ]
        )
    ]
    for load in loads:
        load.start()

    peers = (
        [at(0, j, 0, 0) for j in range(1, X)]
        + [at(1, 0, 0, 0), at(Z - 1, 0, 0, 0)]
        + [at(0, 0, j, 0) for j in range(1, Y)]
        + [at(0, 0, 0, 1)]
    )
    barrier = pltpu.get_barrier_semaphore()
    for peer in peers:
        pl.semaphore_signal(barrier, inc=1, device_id=peer, device_id_type=MESH)

    used = [0]

    def send(src, dst, peer):
        number = used[0]
        used[0] += 1
        return pltpu.make_async_remote_copy(
            src_ref=src,
            dst_ref=dst,
            send_sem=send_sem.at[number],
            recv_sem=recv_sem.at[number],
            device_id=peer,
            device_id_type=MESH,
        )

    def kept(c):
        same = documents[c] == documents[jnp.maximum(c - 1, 0)]
        return jnp.where(same, 1.0, 0.0).astype(F32) * jnp.where(c > 0, 1.0, 0.0).astype(F32)

    def matrix(c):
        return mats[regimes[c]]

    lane_id = lax.broadcasted_iota(jnp.int32, (1, rows), 1)
    lane_mask = [lane_id < HD, lane_id >= HD]
    first = seq * 2

    def tokens(b):
        return slice(b * B, (b + 1) * B)

    def lanes(h):
        return slice(h * N, (h + 1) * N)

    loads[0].wait()
    loads[1].wait()
    for b in range(2):
        flipped = v[tokens(b), :].T
        for h in range(HEADS_DEV):
            part = slice(h * HD, (h + 1) * HD)
            update[b, part, :] = dot(flipped[part], k[tokens(b), lanes(h)], NN)
    loads[2].wait()
    loads[3].wait()
    for b in range(2):
        flipped = g[tokens(b), :].T
        for h in range(HEADS_DEV):
            part = slice(h * HD, (h + 1) * HD)
            source[b, part, :] = dot(flipped[part], q[tokens(b), lanes(h)], NN)
    for load in loads[4:]:
        load.wait()
    row_id = lax.broadcasted_iota(jnp.int32, (rows, 1), 0)
    gamma_rows = jnp.where(row_id < HD, gammas[0], gammas[1])
    keep = [kept(first), kept(first + 1)]
    m0 = matrix(first)
    m1 = matrix(first + 1)
    ahead = update[1] + keep[1] * gamma_rows * turn(update[0], m1, NT)
    behind = source[0] + keep[1] * gamma_rows * turn(source[1], m1, NN)
    behind = keep[0] * gamma_rows * turn(behind, m0, NN)
    for j in range(X):
        for c in range(CHUNKS):
            part = slice(j * piece + c * chunk, j * piece + (c + 1) * chunk)
            t_send[c, j, 0] = ahead[part]
            t_send[c, j, 1] = behind[part]

    pl.semaphore_wait(barrier, len(peers))
    first_round = [
        [send(t_send.at[c, (x + j) % X], t_recv.at[c, x], at(0, j, 0, 0)) for j in far_first(X)]
        for c in range(CHUNKS)
    ]
    for c in range(CHUNKS):
        for copy in first_round[c]:
            copy.start()
        t_recv[c, x] = t_send[c, x]

    def pass_on():
        pl.semaphore_signal(up_sem, inc=1, device_id=at(1, 0, 0, 0), device_id_type=MESH)
        pl.semaphore_signal(down_sem, inc=1, device_id=at(Z - 1, 0, 0, 0), device_id_type=MESH)

    def hear():
        pl.semaphore_wait(up_sem, 1)
        pl.semaphore_wait(down_sem, 1)

    pass_on()

    def pair_product(c):
        return dot(matrix(c + 1), matrix(c), NN)

    base = z * 2 * X
    for j in range(X):
        high, low = split(pair_product(base + 2 * j))
        pairs[j, 0] = high
        pairs[j, 1] = low

    def pair(j):
        return pairs[j, 0], pairs[j, 1]

    def group_product(offset):
        group = (z + offset + Z) % Z
        made = [split(pair_product(group * 2 * X + 2 * j)) for j in range(X)]
        while len(made) > 1:
            made = [split(product(made[i + 1], made[i])) for i in range(0, len(made), 2)]
        return made[0]

    made = pair(0)
    for j in range(1, X):
        made = split(product(pair(j), made))
        inner[0, j - 1, 0] = made[0]
        inner[0, j - 1, 1] = made[1]
    made = pair(X - 1)
    for j in reversed(range(1, X - 1)):
        made = split(product(made, pair(j)))
        inner[1, j - 1, 0] = made[0]
        inner[1, j - 1, 1] = made[1]

    def up_to(j):
        return pair(0) if j == 1 else (inner[0, j - 2, 0], inner[0, j - 2, 1])

    def down_to(j):
        return pair(X - 1) if j == X - 2 else (inner[1, j, 0], inner[1, j, 1])

    hear()
    pass_on()

    gamma = gammas[(x * piece) // HD]
    gamma2 = gamma * gamma
    scale = [gamma2 * kept(base + 2 * j) * kept(base + 2 * j + 1) for j in range(X)]

    gamma_group = jnp.float32(1.0)
    for j in range(X):
        gamma_group = gamma_group * gamma2

    def group_scale(offset):
        group = (z + offset + Z) % Z
        total = gamma_group
        for j in range(2 * X):
            total = total * kept(group * 2 * X + j)
        return total

    own = inner[0, X - 2, 0], inner[0, X - 2, 1]
    own_scale = group_scale(0)
    near, second_round = [], []
    for c in range(CHUNKS):
        for copy in first_round[c]:
            copy.wait()
        run = t_recv[c, X - 1, 0]
        factor = scale[X - 1]
        for j in reversed(range(X - 1)):
            run = run + factor * turn_split(t_recv[c, j, 0], *down_to(j), NT)
            factor = factor * scale[j]
        run_back = t_recv[c, 0, 1]
        factor = scale[0]
        for j in range(1, X):
            run_back = run_back + factor * turn_split(t_recv[c, j, 1], *up_to(j), NN)
            factor = factor * scale[j]
        z_send[c, 0] = run
        z_send[c, 1] = run_back
        near.append(
            [
                send(z_send.at[c, 0], z_fwd.at[c, 0], at(1, 0, 0, 0)),
                send(z_send.at[c, 1], z_bwd.at[c, 0], at(Z - 1, 0, 0, 0)),
            ]
        )
        for copy in near[c]:
            copy.start()
    hear()
    pass_on()
    for c in range(CHUNKS):
        for copy in near[c]:
            copy.wait()
        z_pair[c, 0] = z_send[c, 0] + own_scale * turn_split(z_fwd[c, 0], *own, NT)
        z_pair[c, 1] = z_send[c, 1] + own_scale * turn_split(z_bwd[c, 0], *own, NN)
        second_round.append(
            [
                send(z_pair.at[c, 0], z_fwd.at[c, 2], at(3, 0, 0, 0)),
                send(z_pair.at[c, 1], z_bwd.at[c, 2], at(Z - 3, 0, 0, 0)),
                send(z_pair.at[c, 0], z_fwd.at[c, 1], at(1, 0, 0, 0)),
                send(z_pair.at[c, 1], z_bwd.at[c, 1], at(Z - 1, 0, 0, 0)),
            ]
        )
        for copy in second_round[c]:
            copy.start()

    before, after = [], []
    for c in range(CHUNKS):
        run = t_recv[c, 0, 0]
        run_back = t_recv[c, X - 1, 1]
        fore, back = [None, run], [None] * X
        back[X - 2] = run_back
        for j in range(1, X - 1):
            run = t_recv[c, j, 0] + scale[j] * turn_split(run, *pair(j), NT)
            fore.append(run)
            i = X - 1 - j
            run_back = t_recv[c, i, 1] + scale[i] * turn_split(run_back, *pair(i), NN)
            back[i - 1] = run_back
        before.append(fore)
        after.append(back)
    back = [group_product(-1), group_product(-2)]
    front = [group_product(1), group_product(2)]
    for i, made in enumerate([product(back[0], back[1]), product(front[1], front[0])]):
        groups[i, 0], groups[i, 1] = split(made)

    back_scale = group_scale(-1) * group_scale(-2)
    front_scale = group_scale(1) * group_scale(2)
    third_round = []
    for c in range(CHUNKS):
        for copy in second_round[c]:
            copy.wait()
        inbound = z_fwd[c, 1] + back_scale * turn_split(
            z_fwd[c, 2], groups[0, 0], groups[0, 1], NT
        )
        outbound = z_bwd[c, 1] + front_scale * turn_split(
            z_bwd[c, 2], groups[1, 0], groups[1, 1], NN
        )
        s_send[c, 0, 0] = inbound
        total_scale = scale[0]
        for j in range(1, X):
            s_send[c, j, 0] = before[c][j] + total_scale * turn_split(inbound, *up_to(j), NT)
            total_scale = total_scale * scale[j]
        s_send[c, X - 1, 1] = outbound
        total_scale = scale[X - 1]
        for j in reversed(range(X - 1)):
            s_send[c, j, 1] = after[c][j] + total_scale * turn_split(outbound, *down_to(j), NN)
            total_scale = total_scale * scale[j]
        third_round.append(
            [send(s_send.at[c, (x + j) % X], s_recv.at[c, x], at(0, j, 0, 0)) for j in far_first(X)]
        )
        for copy in third_round[c]:
            copy.start()
        s_recv[c, x] = s_send[c, x]

    row = lax.broadcasted_iota(jnp.int32, (B, B), 0)
    column = lax.broadcasted_iota(jnp.int32, (B, B), 1)
    for b in range(2):
        for h in range(HEADS_DEV):
            q_block = q[tokens(b), lanes(h)]
            k_block = k[tokens(b), lanes(h)]
            v_block = v[tokens(b), :]
            g_block = g[tokens(b), :]
            zero = jnp.zeros_like(g_block)
            g_head = jnp.where(lane_mask[h], g_block, zero)
            probs = jnp.where(row <= column, dot(k_block, q_block, NT), 0.0).astype(BF16)
            scored = jnp.where(row >= column, dot(g_head, v_block, NT), 0.0).astype(BF16)
            turned = jnp.where(row <= column, dot(v_block, g_head, NT), 0.0).astype(BF16)
            q_part[tokens(b), lanes(h)] = dot(scored, k_block, NN)
            k_part[tokens(b), lanes(h)] = dot(turned, q_block, NN)
            if h == 0:
                v_part[tokens(b), :] = dot(probs, g_head, NN)
            else:
                v_part[tokens(b), :] += dot(probs, g_head, NN)

    for copies in third_round:
        for copy in copies:
            copy.wait()

    order = [(c, j) for j in range(X) for c in range(CHUNKS)]
    previous = jnp.concatenate([s_recv[c, j, 0] for c, j in order], axis=0)
    leaving = jnp.concatenate([s_recv[c, j, 1] for c, j in order], axis=0)
    total1 = source[1] + leaving
    entry0 = keep[0] * gamma_rows * turn(previous, m0, NT)
    leave0 = keep[1] * gamma_rows * turn(total1, m1, NN)
    end0 = entry0 + update[0]
    total0 = source[0] + leave0
    for b, (outer, inside) in enumerate([(total0, previous), (total1, end0)]):
        left_high, left_low = split(outer * (keep[b] * gamma_rows))
        right_high, right_low = split(inside)
        term = dot(
            jnp.concatenate([left_high, left_low, left_high], axis=0),
            jnp.concatenate([right_high, right_high, right_low], axis=0),
            TN,
        )
        for j in range(Y * CORES):
            for t in range(PARTS):
                top, left = j * height + t % 2 * part_rows, t // 2 * width
                terms[t, j % CORES, j // CORES, b] = term[
                    top : top + part_rows, left : left + width
                ]
    core_round = [send(terms.at[t, 1 - core], h_core.at[t], at(0, 0, 0, 1)) for t in range(PARTS)]
    for copy in core_round:
        copy.start()

    entry1 = keep[1] * gamma_rows * turn(end0, m1, NT)
    entries = [entry0.astype(BF16), entry1.astype(BF16)]
    leaves = [leave0.astype(BF16), leaving.astype(BF16)]

    y_round = []
    for t in range(PARTS):
        core_round[t].wait()
        for j in range(Y):
            h_sum[t, j] = terms[t, core, j] + h_core[t, j]
        copies = [
            send(h_sum.at[t, (y + j) % Y], h_y.at[t, j - 1], at(0, 0, j, 0)) for j in far_first(Y)
        ]
        for copy in copies:
            copy.start()
        y_round.append(copies)
    x_round = []
    for t in range(PARTS):
        for copy in y_round[t]:
            copy.wait()
        mine = h_sum[t, y]
        for j in range(Y - 1):
            mine = mine + h_y[t, j]
        h_block[t] = mine
        copies = [send(h_block.at[t], h_x.at[t, x], at(0, j, 0, 0)) for j in far_first(X)]
        for copy in copies:
            copy.start()
        x_round.append(copies)
        h_x[t, x] = mine
    chosen = [
        [
            jnp.where(regimes[base + i] == (z + j) % Z * X + x, 1.0, 0.0).astype(F32)
            for i in range(2 * X)
        ]
        for j in range(Z)
    ]
    hear()
    z_round = []
    for t in range(PARTS):
        for copy in x_round[t]:
            copy.wait()
        for j in range(Z):
            total = chosen[j][0] * h_x[t, 0, 0]
            for i in range(1, 2 * X):
                total = total + chosen[j][i] * h_x[t, i // 2, i % 2]
            h_reg[t, j] = total
        copies = [
            send(h_reg.at[t, j], h_z.at[t, j - 1], at(j, 0, 0, 0)) for j in far_first(Z)
        ]
        for copy in copies:
            copy.start()
        z_round.append(copies)

    for b in range(2):
        v_block = v[tokens(b), :]
        g_block = g[tokens(b), :]
        zero = jnp.zeros_like(g_block)
        v_new = v_part[tokens(b), :]
        for h in range(HEADS_DEV):
            g_head = jnp.where(lane_mask[h], g_block, zero)
            v_head = jnp.where(lane_mask[h], v_block, zero)
            qo[tokens(b), lanes(h)] = (
                q_part[tokens(b), lanes(h)] + dot(g_head, entries[b], NN)
            ).astype(BF16)
            ko[tokens(b), lanes(h)] = (
                k_part[tokens(b), lanes(h)] + dot(v_head, leaves[b], NN)
            ).astype(BF16)
            v_new = v_new + jnp.where(
                lane_mask[h], dot(k[tokens(b), lanes(h)], leaves[b], NT), 0.0
            )
        vo[tokens(b), :] = v_new.astype(BF16)

    for t in range(PARTS):
        for copy in z_round[t]:
            copy.wait()
        total = h_reg[t, 0]
        for j in range(Z - 1):
            total = total + h_z[t, j]
        top, left = t % 2 * part_rows, t // 2 * width
        ro[0, top : top + part_rows, left : left + width] = total


def write(*refs):
    count = (len(refs) - 1) // 2
    sem = refs[-1]
    copies = []
    for i in range(count):
        whole = refs[i].shape[0]
        size = whole // 2 if whole > 1 else whole
        for start in range(0, whole, size):
            part = pl.ds(start, size)
            copies.append(pltpu.make_async_copy(refs[i].at[part], refs[count + i].at[part], sem.at[len(copies)]))
    for copy in copies:
        copy.start()
    for copy in copies:
        copy.wait()


def local(Z, Y, queries, keys, values, out_grad, transitions, gammas, regimes, documents):
    tokens_dev = queries.shape[0]
    N = transitions.shape[1]
    rows = values.shape[1]
    HD = rows // HEADS_DEV
    B = tokens_dev // 2
    chunk = rows // X // CHUNKS
    height = N // (Y * CORES)
    anywhere = pl.BlockSpec(memory_space=pl.ANY)
    vmem = pltpu.VMEM
    part_rows, width = height // 2, N // 2
    copies = CHUNKS * (2 * (X - 1) + 6) + PARTS * (1 + (Y - 1) + (X - 1) + 7)
    results = pl.pallas_call(
        functools.partial(kernel, (Z, Y, N, HD, B)),
        out_shape=(
            vmem(queries.shape, BF16),
            vmem(keys.shape, BF16),
            vmem(values.shape, BF16),
            vmem((1, height, N), F32),
        ),
        in_specs=[anywhere] * 8,
        out_specs=[pl.BlockSpec(memory_space=vmem)] * 4,
        scratch_shapes=[
            pltpu.SMEM(regimes.shape, jnp.int32),
            pltpu.SMEM(documents.shape, jnp.int32),
            pltpu.SMEM(gammas.shape, F32),
            vmem(queries.shape, BF16),
            vmem(keys.shape, BF16),
            vmem(values.shape, BF16),
            vmem(values.shape, BF16),
            vmem(transitions.shape, BF16),
            vmem(queries.shape, F32),
            vmem(keys.shape, F32),
            vmem(values.shape, F32),
            vmem((2, rows, N), F32),
            vmem((2, rows, N), F32),
            vmem((X, 2, N, N), BF16),
            vmem((2, 2, N, N), BF16),
            vmem((2, X - 1, 2, N, N), BF16),
            vmem((CHUNKS, X, 2, chunk, N), F32),
            vmem((CHUNKS, X, 2, chunk, N), F32),
            vmem((CHUNKS, 2, chunk, N), F32),
            vmem((CHUNKS, 2, chunk, N), F32),
            vmem((CHUNKS, 3, chunk, N), F32),
            vmem((CHUNKS, 3, chunk, N), F32),
            vmem((CHUNKS, X, 2, chunk, N), F32),
            vmem((CHUNKS, X, 2, chunk, N), F32),
            vmem((PARTS, CORES, Y, 2, part_rows, width), F32),
            vmem((PARTS, Y, 2, part_rows, width), F32),
            vmem((PARTS, Y, 2, part_rows, width), F32),
            vmem((PARTS, Y - 1, 2, part_rows, width), F32),
            vmem((PARTS, 2, part_rows, width), F32),
            vmem((PARTS, X, 2, part_rows, width), F32),
            vmem((PARTS, Z, part_rows, width), F32),
            vmem((PARTS, Z - 1, part_rows, width), F32),
            pltpu.SemaphoreType.REGULAR,
            pltpu.SemaphoreType.REGULAR,
            pltpu.SemaphoreType.DMA((8,)),
            pltpu.SemaphoreType.DMA((copies,)),
            pltpu.SemaphoreType.DMA((copies,)),
        ],
        compiler_params=pltpu.CompilerParams(collective_id=0, has_side_effects=True),
        name="whole",
    )(regimes, documents, gammas, queries, keys, values, out_grad, transitions)
    return pl.pallas_call(
        write,
        out_shape=[jax.ShapeDtypeStruct(result.shape, result.dtype) for result in results],
        in_specs=[anywhere] * 4,
        out_specs=[anywhere] * 4,
        scratch_shapes=[pltpu.SemaphoreType.DMA((7,))],
        compiler_params=pltpu.CompilerParams(vmem_limit_bytes=1 << 20),
        name="write",
    )(*results)


def solution(mesh):
    in_specs = (
        P("seq", "head"),
        P("seq", "head"),
        P("seq", "head"),
        P("seq", "head"),
        P(),
        P("head"),
        P(),
        P(),
    )
    out_specs = (P("seq", "head"), P("seq", "head"), P("seq", "head"), P("seq", "head", None))
    body = functools.partial(local, mesh.shape["seq"] // X, mesh.shape["head"] // CORES)
    return jax.shard_map(body, mesh=mesh, in_specs=in_specs, out_specs=out_specs, check_vma=False)
```
